128 devices in a mesh: dom: 16 (over y, x), sub: 8 (over z, core).
Axes of the slice: x: 4, y: 4, z: 4, core: 2. Of those that a mesh axis runs over, the one named last changes fastest.
Arguments:
- old_coef: float32 [100, 524288], P(None, ('dom', 'sub')), may hold values from -6 to 6
- old_index: int32 [1048576], P(('dom', 'sub')), may hold values from 0 to 4095
- pair_count: int32 [128, 128], replicated, may hold values from 16 to 64, as said below
- new_index: int32 [1048576], P(('dom', 'sub')), may hold values from 0 to 2047
- old_points: float32 [3, 25165824], P(None, ('dom', 'sub')), may hold values from 0 to 1
- new_points: float32 [3, 25165824], P(None, ('dom', 'sub')), may hold values from 0 to 1
- weights: float32 [25165824], P(('dom', 'sub')), may hold values from 0.1 to 1
- jacobian: float32 [262144], P(('dom', 'sub')), may hold values from 0.5 to 2
- minv_ref: float32 [20, 20], replicated, may hold values from -0.06 to 2.5, as said below
- send_order: int32 [128, 2048], P(('dom', 'sub')), may hold values from 0 to 2047, each once within a row
Outputs:
- solver_coef: float32 [100, 262144], P(None, ('dom', 'sub'))
The draws below stay inside these ranges and needn't reach their ends.
Inputs may be any that keep to these rules, and one draw needn't show every extreme that they name: `pair_count`: entry (s, d) is how many of the 64 slots from s to d are used, the first ones; each row has an entry equal to 64, and one column is 64 in every row. `minv_ref`: symmetric with a dominant diagonal. `send_order`: each row is a permutation.
All inputs are finite; a program needn't handle non-finite values.
Results may differ from the reference program's by a relative error of at most 0.0003.
Values sent between devices are 32-bit elements; how exact they have to be, the bound alone decides.
No kernel may reach another device: no remote copies, remote signals or barrier semaphores. Data moves between devices by JAX's collectives and lax.ppermute only.
A program may use at most 192 MiB of HBM per device.

```python
import math
import jax
import jax.numpy as jnp
from jax import lax

VARS = 5
MODES = 20
QUAD = 24
E_DEV = 4096
N_DEV = 2048
CAP = 64
SLOTS_DEV = 8192
E_OLD = 524288
N_NEW = 262144
SHARE = 16
DEVICES = 128


def draw_pair_count(key, part):
    key_counts = jax.random.fold_in(key, 11)
    key_peak = jax.random.fold_in(key, 12)
    key_heavy = jax.random.fold_in(key, 13)
    counts = jax.random.randint(key_counts, (DEVICES, DEVICES), CAP // 4, CAP + 1)
    row_peak = jax.random.randint(key_peak, (DEVICES,), 0, DEVICES)
    heavy_column = jax.random.randint(key_heavy, (), 0, DEVICES)
    columns = jnp.arange(DEVICES)
    full = (columns[None, :] == row_peak[:, None]) | (columns[None, :] == heavy_column)
    return jnp.where(full, CAP, counts).astype(jnp.int32)


def draw_minv_ref(key, part):
    key_diag = jax.random.fold_in(key, 21)
    key_off = jax.random.fold_in(key, 22)
    diagonal = jax.random.uniform(key_diag, (MODES,), jnp.float32, 1.5, 2.5)
    offdiag = jax.random.uniform(key_off, (MODES, MODES), jnp.float32, -0.06, 0.06)
    offdiag = (offdiag + offdiag.T) * 0.5
    identity = jnp.eye(MODES, dtype=jnp.float32)
    return offdiag * (1.0 - identity) + identity * diagonal[None, :]


def plant(entries, own_key, least, top_value):
    index_at = [jax.random.randint(jax.random.fold_in(own_key, axis), (), 0, length) for axis, length in enumerate(entries.shape)]
    widest = entries.shape.index(max(entries.shape))
    next_to = index_at[:widest] + [(index_at[widest] + 1) % entries.shape[widest]] + index_at[widest + 1:]
    return entries.at[tuple(index_at)].set(least).at[tuple(next_to)].set(top_value)


def block_levels(own_key, dims, shards, least, top_value):
    def one(axis_at, parts):
        draws = jax.random.uniform(jax.random.fold_in(jax.random.fold_in(own_key, 6), axis_at), (parts,), jnp.float32, least / len(shards), top_value / len(shards))
        return jnp.repeat(jnp.exp(draws), dims[axis_at] // parts).reshape((-1,) + (1,) * (len(dims) - axis_at - 1))

    gain = one(*shards[0])
    for cut in shards[1:]:
        gain = gain * one(*cut)
    return gain


def bell_draw(stream_key, shape, spread, most, shards=(), kind=jnp.bfloat16):
    result = jax.random.normal(stream_key, shape, jnp.float32) * spread
    if len(shards) > 0:
        result = block_levels(stream_key, shape, shards, -0.22, 0.18) * result
    return jnp.clip(result, min=-most, max=most).astype(kind)


def setup_inputs(seed: int = 0) -> dict:
    arg_keys = jax.random.split(jax.random.key(seed), 11)
    old_coef = bell_draw(arg_keys[0], (VARS * MODES, E_OLD), 1.0, 6.0, ((1, 128),), jnp.float32)
    old_index = plant(jax.random.randint(arg_keys[1], (DEVICES * DEVICES * CAP,), 0, E_DEV), jax.random.fold_in(arg_keys[1], 1), 0, E_DEV - 1).astype(jnp.int32)
    pair_count = draw_pair_count(jax.random.fold_in(arg_keys[10], 71), 0)
    new_index = plant(jax.random.randint(arg_keys[3], (DEVICES * DEVICES * CAP,), 0, N_DEV), jax.random.fold_in(arg_keys[3], 1), 0, N_DEV - 1).astype(jnp.int32)
    old_points = jnp.clip(1.0 * jax.random.uniform(arg_keys[4], (3, DEVICES * QUAD * SLOTS_DEV), jnp.float32) ** block_levels(arg_keys[4], (3, DEVICES * QUAD * SLOTS_DEV), ((1, 128),), -0.2, 0.2), 0.0, 1.0)
    new_points = jnp.clip(1.0 * jax.random.uniform(arg_keys[5], (3, DEVICES * QUAD * SLOTS_DEV), jnp.float32) ** block_levels(arg_keys[5], (3, DEVICES * QUAD * SLOTS_DEV), ((1, 128),), -0.2, 0.2), 0.0, 1.0)
    weights = jnp.clip(jnp.exp(math.log(1.0) - 2.3025851 * jax.random.uniform(arg_keys[6], (DEVICES * QUAD * SLOTS_DEV,), jnp.float32) ** block_levels(arg_keys[6], (DEVICES * QUAD * SLOTS_DEV,), ((0, 128),), -0.2, 0.2)), 0.1, 1.0)
    jacobian = jnp.clip(jnp.exp(math.log(2.0) - 1.3862944 * jax.random.uniform(arg_keys[7], (N_NEW,), jnp.float32) ** block_levels(arg_keys[7], (N_NEW,), ((0, 128),), -0.2, 0.2)), 0.5, 2.0)
    minv_ref = draw_minv_ref(jax.random.fold_in(arg_keys[10], 71), 0)
    send_order = jax.vmap(lambda own: jax.random.permutation(own, N_DEV))(jax.random.split(arg_keys[9], DEVICES)).reshape((DEVICES, N_DEV)).astype(jnp.int32)
    return {"old_coef": old_coef, "old_index": old_index, "pair_count": pair_count, "new_index": new_index, "old_points": old_points, "new_points": new_points, "weights": weights, "jacobian": jacobian, "minv_ref": minv_ref, "send_order": send_order}


def modal_basis(points):
    first, second, third = points[0], points[1], points[2]
    unit = jnp.ones_like(first)
    first_pow = [unit, first, first * first, first * first * first]
    second_pow = [unit, second, second * second, second * second * second]
    third_pow = [unit, third, third * third, third * third * third]
    rows = []
    for degree in range(4):
        for power_a in range(degree, -1, -1):
            for power_b in range(degree - power_a, -1, -1):
                rows.append(first_pow[power_a] * second_pow[power_b] * third_pow[degree - power_a - power_b])
    return jnp.stack(rows)


def reference(old_coef, old_index, pair_count, new_index, old_points, new_points, weights, jacobian, minv_ref, send_order):
    total_rows = VARS * MODES
    slots = SLOTS_DEV
    old_lists = old_index.reshape(DEVICES, DEVICES, CAP)
    sources = jnp.arange(DEVICES).astype(jnp.int32)

    def receive(dest):
        local_idx = old_lists[:, dest, :]
        global_idx = (sources[:, None] * E_DEV + local_idx).reshape(-1).astype(jnp.int32)
        live = (jnp.arange(CAP).astype(jnp.int32)[None, :] < pair_count[:, dest][:, None]).reshape(-1)
        coefs = jnp.where(live[None, :], jnp.take(old_coef, global_idx, axis=1), 0.0)
        start = (dest * QUAD * slots).astype(jnp.int32)
        pts_old = lax.dynamic_slice_in_dim(old_points, start, QUAD * slots, 1).reshape(3, QUAD, slots)
        pts_new = lax.dynamic_slice_in_dim(new_points, start, QUAD * slots, 1).reshape(3, QUAD, slots)
        wts = lax.dynamic_slice_in_dim(weights, start, QUAD * slots, 0).reshape(QUAD, slots)
        targets = lax.dynamic_slice_in_dim(new_index, (dest * slots).astype(jnp.int32), slots, 0)
        jac = lax.dynamic_slice_in_dim(jacobian, (dest * N_DEV).astype(jnp.int32), N_DEV, 0)
        psi_old = modal_basis(pts_old)
        psi_new = modal_basis(pts_new)
        values = jnp.einsum("vks,kqs->vqs", coefs.reshape(VARS, MODES, slots), psi_old, precision=lax.Precision.HIGHEST)
        weighted = values * wts[None]
        moments = jnp.einsum("mqs,vqs->vms", psi_new, weighted, precision=lax.Precision.HIGHEST).reshape(total_rows, slots)
        rhs = jnp.zeros((total_rows, N_DEV), jnp.float32).at[:, targets].add(moments)
        proj = jnp.einsum("mk,vkf->vmf", minv_ref, rhs.reshape(VARS, MODES, N_DEV), precision=lax.Precision.HIGHEST)
        return (proj / jac[None, None, :]).reshape(total_rows, N_DEV)

    projected = lax.map(receive, sources)
    ordered = jnp.take_along_axis(projected, send_order[:, None, :], axis=2)
    ordered = ordered.reshape(DEVICES, total_rows, DEVICES, SHARE)
    ordered = jnp.transpose(ordered, (1, 2, 0, 3))
    return ordered.reshape(total_rows, DEVICES * N_DEV)
```

```python
import functools
import jax
import jax.numpy as jnp
from jax import lax
from jax.experimental import pallas as pl
from jax.experimental.pallas import tpu as pltpu
from jax.sharding import PartitionSpec as P

VARS = 5
MODES = 20
ROWS = 100
HALF = 50
QUAD = 24
CAP = 64
LANES = 128


def gather_kernel(idx_ref, cnt_ref, coef_ref, out_ref, tab_ref, buf0, buf1):
    width = coef_ref.shape[1]
    pad = jnp.zeros((64 - HALF, LANES), jnp.float32)

    def build(j, carry):
        start = pl.multiple_of(j * LANES, LANES)
        block = coef_ref[:, pl.ds(start, LANES)]
        wide = jnp.concatenate([block[:HALF], pad, block[HALF:], pad], axis=0)
        tab_ref[pl.ds(start, LANES), :] = wide.T
        return carry

    lax.fori_loop(0, width // LANES, build, 0, unroll=2)
    lane = lax.broadcasted_iota(jnp.int32, (1, LANES), 1)
    low = lane < 64

    def fetch(pair, buf):
        for j in range(LANES):
            buf[pl.ds(j, 1), :] = tab_ref[pl.ds(idx_ref[pair * LANES + j], 1), :]

    def emit(pair, buf, base, shift):
        limit = jnp.where(low, cnt_ref[2 * pair], cnt_ref[2 * pair + 1] + 64)
        turned = buf[...].T
        live = lane < limit
        first = jnp.where(live, turned[:HALF], 0.0)
        second = jnp.where(live, turned[64 : 64 + HALF], 0.0)
        first_r = pltpu.roll(first, 64, 1)
        second_r = pltpu.roll(second, 64, 1)
        out_ref[pl.ds(base + shift, HALF), :] = jnp.where(low, first, second_r)
        out_ref[pl.ds(base + shift + HALF, HALF), :] = jnp.where(low, first_r, second)

    pairs = idx_ref.shape[0] // LANES
    fetch(0, buf0)

    def step(turn, carry):
        base = pl.multiple_of(turn * 200, 8)
        fetch(2 * turn + 1, buf1)
        emit(2 * turn, buf0, base, 0)
        fetch(jnp.minimum(2 * turn + 2, pairs - 1), buf0)
        emit(2 * turn + 1, buf1, base, 100)
        return carry

    lax.fori_loop(0, pairs // 2, step, 0)


def gather(old_coef, old_index, counts):
    slots = old_index.shape[0]
    width = old_coef.shape[1]
    return pl.pallas_call(
        gather_kernel,
        out_shape=jax.ShapeDtypeStruct((slots // CAP * HALF, LANES), jnp.float32),
        in_specs=[
            pl.BlockSpec(memory_space=pltpu.SMEM),
            pl.BlockSpec(memory_space=pltpu.SMEM),
            pl.BlockSpec(memory_space=pltpu.VMEM),
        ],
        out_specs=pl.BlockSpec(memory_space=pltpu.VMEM),
        scratch_shapes=[
            pltpu.VMEM((width, LANES), jnp.float32),
            pltpu.VMEM((LANES, LANES), jnp.float32),
            pltpu.VMEM((LANES, LANES), jnp.float32),
        ],
        name="gather",
    )(old_index, counts, old_coef)


def monomials(first, second, third):
    unit = None
    fp = [unit, first, first * first]
    fp.append(fp[2] * first)
    sp = [unit, second, second * second]
    sp.append(sp[2] * second)
    tp = [unit, third, third * third]
    tp.append(tp[2] * third)
    rows = []
    for degree in range(4):
        for a in range(degree, -1, -1):
            for b in range(degree - a, -1, -1):
                out = None
                for term in (fp[a], sp[b], tp[degree - a - b]):
                    if term is not None:
                        out = term if out is None else out * term
                rows.append(out)
    return rows


def moment_kernel(old_ref, new_ref, w_ref, out_ref, po_ref, pn_ref):
    def basis(q, carry):
        weight = w_ref[q]
        old = monomials(old_ref[0, q], old_ref[1, q], old_ref[2, q])
        new = monomials(new_ref[0, q], new_ref[1, q], new_ref[2, q])
        for k in range(MODES):
            po_ref[q, k] = weight if k == 0 else old[k] * weight
            if k > 0:
                pn_ref[q, k] = new[k]
        return carry

    lax.fori_loop(0, QUAD, basis, 0)
    tile = 5
    zero = jnp.zeros((8, LANES), jnp.float32)
    for m0 in range(0, MODES, tile):
        for k0 in range(0, MODES, tile):

            def add(q, accs):
                left = [None if m0 + i == 0 else pn_ref[q, m0 + i] for i in range(tile)]
                right = [po_ref[q, k0 + j] for j in range(tile)]
                return tuple(
                    accs[i * tile + j] + (right[j] if left[i] is None else left[i] * right[j])
                    for i in range(tile)
                    for j in range(tile)
                )

            accs = lax.fori_loop(0, QUAD, add, (zero,) * (tile * tile), unroll=4)
            for i in range(tile):
                for j in range(tile):
                    out_ref[0, (m0 + i) * MODES + k0 + j] = accs[i * tile + j]


def moment_matrix(old_points, new_points, weights):
    groups = weights.shape[0] // QUAD // LANES
    blocks = groups // 8
    shape = (3, QUAD, groups, LANES)
    return pl.pallas_call(
        moment_kernel,
        grid=(blocks,),
        out_shape=jax.ShapeDtypeStruct((blocks, MODES * MODES, 8, LANES), jnp.float32),
        in_specs=[
            pl.BlockSpec((3, QUAD, 8, LANES), lambda i: (0, 0, i, 0)),
            pl.BlockSpec((3, QUAD, 8, LANES), lambda i: (0, 0, i, 0)),
            pl.BlockSpec((QUAD, 8, LANES), lambda i: (0, i, 0)),
        ],
        out_specs=pl.BlockSpec((1, MODES * MODES, 8, LANES), lambda i: (i, 0, 0, 0)),
        scratch_shapes=[
            pltpu.VMEM((QUAD, MODES, 8, LANES), jnp.float32),
            pltpu.VMEM((QUAD, MODES, 8, LANES), jnp.float32),
        ],
        cost_estimate=pl.CostEstimate(
            flops=int(20e-6 * 1.1e15), bytes_accessed=40 * 2**20, transcendentals=0
        ),
        name="moment_matrix",
    )(old_points.reshape(shape), new_points.reshape(shape), weights.reshape(shape[1:]))


def index_kernel(order_s, index_ref, jac_ref, target_ref, jacp_ref, order_ref):
    rows = jac_ref.shape[0]
    place = lax.broadcasted_iota(jnp.int32, (rows, LANES), 0) * LANES + lax.broadcasted_iota(
        jnp.int32, (rows, LANES), 1
    )

    def invert(p, inverse):
        return jnp.where(place == order_s[p], p, inverse)

    inverse = lax.fori_loop(
        0, rows * LANES, invert, jnp.zeros((rows, LANES), jnp.int32), unroll=8
    )

    def look(table, index):
        low = index & (LANES - 1)
        high = index >> 7
        found = jnp.zeros(index.shape, table.dtype)
        for r in range(rows):
            row = jnp.broadcast_to(table[r : r + 1], index.shape)
            found = jnp.where(high == r, jnp.take_along_axis(row, low, axis=1), found)
        return found

    for g in range(index_ref.shape[0] // 8):
        target_ref[8 * g : 8 * g + 8, :] = look(inverse, index_ref[8 * g : 8 * g + 8, :])
    jac = jac_ref[...]
    for g in range(rows // 8):
        jacp_ref[8 * g : 8 * g + 8, :] = look(jac, order_ref[8 * g : 8 * g + 8, :])


def index_tables(order, new_index, jacobian):
    slots = new_index.shape[0]
    count = order.shape[0]
    vm = pl.BlockSpec(memory_space=pltpu.VMEM)
    return pl.pallas_call(
        lambda s, i, j, o, t, jp: index_kernel(s, i, j, t, jp, o),
        out_shape=(
            jax.ShapeDtypeStruct((slots // LANES, LANES), jnp.int32),
            jax.ShapeDtypeStruct((count // LANES, LANES), jnp.float32),
        ),
        in_specs=[pl.BlockSpec(memory_space=pltpu.SMEM), vm, vm, vm],
        out_specs=(vm, vm),
        cost_estimate=pl.CostEstimate(
            flops=int(4e-6 * 1.1e15), bytes_accessed=8 * 2**20, transcendentals=0
        ),
        name="index_tables",
    )(
        order,
        new_index.reshape(-1, LANES),
        jacobian.reshape(-1, LANES),
        order.reshape(-1, LANES),
    )


PADF = 104
BINS = 512


def project_kernel(
    recv_ref, m_ref, target_ref, minv_ref, jac_ref, out_ref, coef_ref, y_ref, lhs_ref, acc_ref
):
    turn = pl.program_id(0)
    folds = acc_ref.shape[0] // (2 * PADF)

    @pl.when(turn == 0)
    def _():
        acc_ref[...] = jnp.zeros_like(acc_ref)
        y_ref[...] = jnp.zeros_like(y_ref)

    lane = lax.broadcasted_iota(jnp.int32, (8, LANES), 1)
    low = lane < 64
    for r in range(HALF):
        even = recv_ref[pl.ds(r, 8, stride=2 * HALF), :]
        odd = recv_ref[pl.ds(HALF + r, 8, stride=2 * HALF), :]
        coef_ref[r] = jnp.where(low, even, pltpu.roll(odd, 64, 1))
        coef_ref[r + HALF] = jnp.where(low, pltpu.roll(even, 64, 1), odd)
    tile = 4
    for m0 in range(0, MODES, tile):
        accs = [None] * (tile * VARS)
        for k in range(MODES):
            coefs = [coef_ref[v * MODES + k] for v in range(VARS)]
            for i in range(tile):
                entry = m_ref[0, (m0 + i) * MODES + k]
                for v in range(VARS):
                    term = entry * coefs[v]
                    old = accs[i * VARS + v]
                    accs[i * VARS + v] = term if old is None else old + term
        for i in range(tile):
            for v in range(VARS):
                f = v * MODES + m0 + i
                y_ref[pl.ds((f // 8) * 64 + f % 8, 8, stride=8), :] = accs[i * VARS + v]
    slots = 8 * LANES
    rows = []
    for fb in range(PADF // 8):
        rows.append(
            jnp.concatenate(
                [y_ref[(fb * 8 + g) * 8 : (fb * 8 + g) * 8 + 8, :] for g in range(8)], axis=1
            )
        )
    y = jnp.concatenate(rows, axis=0)
    high = y.astype(jnp.bfloat16)
    rest = y - high.astype(jnp.float32)
    both = jnp.concatenate([high.astype(jnp.float32), rest], axis=0).astype(jnp.bfloat16)
    target = jnp.concatenate([target_ref[g : g + 1, :] for g in range(8)], axis=1)
    fold = target // BINS
    for a in range(folds):
        keep = jnp.where(fold == a, 1.0, 0.0).astype(jnp.bfloat16)
        lhs_ref[a * 2 * PADF : (a + 1) * 2 * PADF, :] = both * keep
    bins = lax.broadcasted_iota(jnp.int32, (BINS, slots), 0)
    onehot = jnp.where(bins == (target & (BINS - 1)), 1.0, 0.0).astype(jnp.bfloat16)
    acc_ref[...] += lax.dot_general(
        lhs_ref[...], onehot, (((1,), (1,)), ((), ())), preferred_element_type=jnp.float32
    )

    @pl.when(turn == pl.num_programs(0) - 1)
    def _():
        for a in range(folds):
            base = a * 2 * PADF
            rhs = acc_ref[base : base + PADF, :] + acc_ref[base + PADF : base + 2 * PADF, :]
            done = jnp.dot(
                minv_ref[...],
                rhs,
                precision=lax.Precision.HIGHEST,
                preferred_element_type=jnp.float32,
            )
            done = done / jac_ref[:, a * BINS : (a + 1) * BINS]
            for j in range(BINS // LANES):
                out_ref[a * BINS + j * LANES : a * BINS + (j + 1) * LANES, :] = done[
                    :, j * LANES : (j + 1) * LANES
                ].T


def project(received, matrix, target, minv, jac):
    blocks = matrix.shape[0]
    count = jac.shape[1]
    rows = received.shape[0] // blocks
    folds = count // BINS
    return pl.pallas_call(
        project_kernel,
        grid=(blocks,),
        out_shape=jax.ShapeDtypeStruct((count, LANES), jnp.float32),
        in_specs=[
            pl.BlockSpec((rows, LANES), lambda i: (i, 0)),
            pl.BlockSpec((1, MODES * MODES, 8, LANES), lambda i: (i, 0, 0, 0)),
            pl.BlockSpec((8, LANES), lambda i: (i, 0)),
            pl.BlockSpec((LANES, PADF), lambda i: (0, 0)),
            pl.BlockSpec((1, count), lambda i: (0, 0)),
        ],
        out_specs=pl.BlockSpec((count, LANES), lambda i: (0, 0)),
        scratch_shapes=[
            pltpu.VMEM((ROWS, 8, LANES), jnp.float32),
            pltpu.VMEM((PADF * 8, LANES), jnp.float32),
            pltpu.VMEM((folds * 2 * PADF, 8 * LANES), jnp.bfloat16),
            pltpu.VMEM((folds * 2 * PADF, BINS), jnp.float32),
        ],
        name="project",
    )(received, matrix, target, minv, jac)


def local(old_coef, old_index, pair_count, new_index, old_points, new_points, weights, jacobian,
          minv_ref, send_order):
    axes = ("dom", "sub")
    devices = lax.axis_size(axes)
    myself = lax.axis_index(axes)
    counts = lax.dynamic_slice_in_dim(pair_count, myself, 1, 0)[0]
    outgoing = gather(old_coef, old_index, counts)
    outgoing = outgoing.reshape(devices, HALF // 2, 2, LANES)
    received = lax.all_to_all(outgoing, axes, split_axis=0, concat_axis=0, tiled=True)
    received = received.reshape(devices * HALF, LANES)
    matrix = moment_matrix(old_points, new_points, weights)
    target, jac = index_tables(send_order[0], new_index, jacobian)
    minv = jnp.pad(jnp.kron(jnp.eye(VARS, dtype=jnp.float32), minv_ref), ((0, 28), (0, 4)))
    leaving = project(received, matrix, target, minv, jac.reshape(1, -1))
    leaving = leaving.reshape(devices, -1, LANES)
    arrived = lax.all_to_all(leaving, axes, split_axis=0, concat_axis=0, tiled=True)
    return arrived.reshape(-1, LANES)[:, :ROWS].T


def solution(mesh):
    placed = (
        P(None, ("dom", "sub")),
        P(("dom", "sub")),
        P(),
        P(("dom", "sub")),
        P(None, ("dom", "sub")),
        P(None, ("dom", "sub")),
        P(("dom", "sub")),
        P(("dom", "sub")),
        P(),
        P(("dom", "sub"), None),
    )
    return jax.shard_map(
        local, mesh=mesh, in_specs=placed, out_specs=P(None, ("dom", "sub")), check_vma=False
    )
```

```python
import functools
import jax
import jax.numpy as jnp
from jax import lax
from jax.experimental import pallas as pl
from jax.experimental.pallas import tpu as pltpu
from jax.sharding import PartitionSpec as P

VARS = 5
MODES = 20
ROWS = 100
HALF = 50
QUAD = 24
CAP = 64
LANES = 128


def gather_kernel(idx_ref, cnt_ref, coef_ref, out_ref, tab_ref, buf_ref):
    part = pl.program_id(0)
    width = coef_ref.shape[1]
    pairs = buf_ref.shape[0] // LANES
    lane = lax.broadcasted_iota(jnp.int32, (1, LANES), 1)
    low = lane < 64

    @pl.when(part == 0)
    def _():
        pad = jnp.zeros((64 - HALF, LANES), jnp.float32)

        def build(j, carry):
            start = pl.multiple_of(j * LANES, LANES)
            block = coef_ref[:, pl.ds(start, LANES)]
            wide = jnp.concatenate([block[:HALF], pad, block[HALF:], pad], axis=0)
            tab_ref[pl.ds(start, LANES), :] = wide.T
            return carry

        lax.fori_loop(0, width // LANES, build, 0, unroll=4)

    def fetch(t, carry):
        base = pl.multiple_of(t * LANES, LANES)
        first = (part * pairs + t) * LANES
        for j in range(LANES):
            buf_ref[pl.ds(base + j, 1), :] = tab_ref[pl.ds(idx_ref[first + j], 1), :]
        return carry

    lax.fori_loop(0, pairs, fetch, 0)

    turned = [buf_ref[u * LANES : (u + 1) * LANES, :].T for u in range(pairs)]
    for u in range(pairs):
        pair = part * pairs + u
        limit = jnp.where(low, cnt_ref[2 * pair], cnt_ref[2 * pair + 1] + 64)
        live = lane < limit
        first = jnp.where(live, turned[u][:HALF], 0.0)
        second = jnp.where(live, turned[u][64 : 64 + HALF], 0.0)
        out_ref[u * ROWS : u * ROWS + HALF, :] = jnp.where(low, first, pltpu.roll(second, 64, 1))
        out_ref[u * ROWS + HALF : (u + 1) * ROWS, :] = jnp.where(
            low, pltpu.roll(first, 64, 1), second
        )


def gather(old_coef, old_index, counts, steps=4):
    slots = old_index.shape[0]
    rows, width = old_coef.shape
    total = slots // CAP * HALF
    return pl.pallas_call(
        gather_kernel,
        grid=(steps,),
        out_shape=jax.ShapeDtypeStruct((total, LANES), jnp.float32),
        in_specs=[
            pl.BlockSpec(memory_space=pltpu.SMEM),
            pl.BlockSpec(memory_space=pltpu.SMEM),
            pl.BlockSpec((rows, width), lambda i: (0, 0), pipeline_mode=pl.Buffered(1)),
        ],
        out_specs=pl.BlockSpec((total // steps, LANES), lambda i: (i, 0)),
        scratch_shapes=[
            pltpu.VMEM((width, LANES), jnp.float32),
            pltpu.VMEM((slots // steps, LANES), jnp.float32),
        ],
        name="gather",
    )(old_index, counts, old_coef)


def monomials(first, second, third):
    unit = None
    fp = [unit, first, first * first]
    fp.append(fp[2] * first)
    sp = [unit, second, second * second]
    sp.append(sp[2] * second)
    tp = [unit, third, third * third]
    tp.append(tp[2] * third)
    rows = []
    for degree in range(4):
        for a in range(degree, -1, -1):
            for b in range(degree - a, -1, -1):
                out = None
                for term in (fp[a], sp[b], tp[degree - a - b]):
                    if term is not None:
                        out = term if out is None else out * term
                rows.append(out)
    return rows


def moment_kernel(old_ref, new_ref, w_ref, out_ref, po_ref, pn_ref):
    def basis(q, carry):
        weight = w_ref[q]
        old = monomials(*[old_ref[a, q] for a in range(3)])
        new = monomials(*[new_ref[a, q] for a in range(3)])
        for k in range(1, MODES):
            pn_ref[q, k] = new[k] * weight
            if k > 3:
                po_ref[q, k] = old[k]
        return carry

    lax.fori_loop(0, QUAD, basis, 0, unroll=2)
    tile = 5
    zero = jnp.zeros((8, LANES), jnp.float32)

    def weighted(q, m):
        return w_ref[q] if m == 0 else pn_ref[q, m]

    def plain(q, k):
        if k == 0:
            return None
        return old_ref[k - 1, q] if k < 4 else po_ref[q, k]

    for m0 in range(0, MODES, tile):
        for k0 in range(0, MODES, tile):

            def add(q, accs):
                left = [weighted(q, m0 + i) for i in range(tile)]
                right = [plain(q, k0 + j) for j in range(tile)]
                return tuple(
                    accs[i * tile + j] + (left[i] if right[j] is None else left[i] * right[j])
                    for i in range(tile)
                    for j in range(tile)
                )

            accs = lax.fori_loop(0, QUAD, add, (zero,) * (tile * tile), unroll=12)
            for i in range(tile):
                for j in range(tile):
                    out_ref[0, (m0 + i) * MODES + k0 + j] = accs[i * tile + j]


def moment_matrix(old_points, new_points, weights):
    groups = weights.shape[0] // QUAD // LANES
    blocks = groups // 8
    shape = (3, QUAD, groups, LANES)
    return pl.pallas_call(
        moment_kernel,
        grid=(blocks,),
        out_shape=jax.ShapeDtypeStruct((blocks, MODES * MODES, 8, LANES), jnp.float32),
        in_specs=[
            pl.BlockSpec((3, QUAD, 8, LANES), lambda i: (0, 0, i, 0)),
            pl.BlockSpec((3, QUAD, 8, LANES), lambda i: (0, 0, i, 0)),
            pl.BlockSpec((QUAD, 8, LANES), lambda i: (0, i, 0)),
        ],
        out_specs=pl.BlockSpec((1, MODES * MODES, 8, LANES), lambda i: (i, 0, 0, 0)),
        scratch_shapes=[
            pltpu.VMEM((QUAD, MODES, 8, LANES), jnp.float32),
            pltpu.VMEM((QUAD, MODES, 8, LANES), jnp.float32),
        ],
        cost_estimate=pl.CostEstimate(
            flops=int(20e-6 * 1.1e15), bytes_accessed=40 * 2**20, transcendentals=0
        ),
        name="moment_matrix",
    )(old_points.reshape(shape), new_points.reshape(shape), weights.reshape(shape[1:]))


def index_kernel(order_s, index_ref, jac_ref, order_ref, minv_ref, target_ref, jacp_ref, wide_ref):
    wide_ref[...] = jnp.zeros_like(wide_ref)
    for v in range(VARS):
        wide_ref[v * MODES : (v + 1) * MODES, v * MODES : (v + 1) * MODES] = minv_ref[...]
    rows = jac_ref.shape[0]
    place = lax.broadcasted_iota(jnp.int32, (rows, LANES), 0) * LANES + lax.broadcasted_iota(
        jnp.int32, (rows, LANES), 1
    )

    def invert(p, inverse):
        return jnp.where(place == order_s[p], p, inverse)

    inverse = lax.fori_loop(
        0, rows * LANES, invert, jnp.zeros((rows, LANES), jnp.int32), unroll=8
    )

    def look(table, index):
        low = index & (LANES - 1)
        high = index >> 7
        found = jnp.zeros(index.shape, table.dtype)
        for r in range(rows):
            row = jnp.broadcast_to(table[r : r + 1], index.shape)
            found = jnp.where(high == r, jnp.take_along_axis(row, low, axis=1), found)
        return found

    for g in range(index_ref.shape[0] // 8):
        target_ref[8 * g : 8 * g + 8, :] = look(inverse, index_ref[8 * g : 8 * g + 8, :])
    jac = jac_ref[...]
    for g in range(rows // 8):
        jacp_ref[8 * g : 8 * g + 8, :] = look(jac, order_ref[8 * g : 8 * g + 8, :])


def index_tables(order, new_index, jacobian, minv):
    slots = new_index.shape[0]
    count = order.shape[0]
    vm = pl.BlockSpec(memory_space=pltpu.VMEM)
    return pl.pallas_call(
        index_kernel,
        out_shape=(
            jax.ShapeDtypeStruct((slots // LANES, LANES), jnp.int32),
            jax.ShapeDtypeStruct((count // LANES, LANES), jnp.float32),
            jax.ShapeDtypeStruct((LANES, PADF), jnp.float32),
        ),
        in_specs=[pl.BlockSpec(memory_space=pltpu.SMEM), vm, vm, vm, vm],
        out_specs=(vm, vm, vm),
        cost_estimate=pl.CostEstimate(
            flops=int(4e-6 * 1.1e15), bytes_accessed=8 * 2**20, transcendentals=0
        ),
        name="index_tables",
    )(
        order,
        new_index.reshape(-1, LANES),
        jacobian.reshape(-1, LANES),
        order.reshape(-1, LANES),
        minv,
    )


PADF = 104
BINS = 512


def project_kernel(
    recv_ref, m_ref, target_ref, minv_ref, jac_ref, out_ref, coef_ref, y_ref, lhs_ref, acc_ref
):
    turn = pl.program_id(0)
    folds = acc_ref.shape[0] // (2 * PADF)
    half = jnp.bfloat16
    single = jnp.float32

    @pl.when(turn == 0)
    def _():
        acc_ref[...] = jnp.zeros_like(acc_ref)
        y_ref[...] = jnp.zeros_like(y_ref)

    low = lax.broadcasted_iota(jnp.int32, (8, LANES), 1) < 64
    first = pl.multiple_of(turn * (8 * ROWS), 8)
    for r in range(HALF):
        even = recv_ref[pl.ds(first + r, 8, stride=ROWS), :]
        odd = recv_ref[pl.ds(first + HALF + r, 8, stride=ROWS), :]
        coef_ref[r] = jnp.where(low, even, pltpu.roll(odd, 64, 1))
        coef_ref[r + HALF] = jnp.where(low, pltpu.roll(even, 64, 1), odd)
    tile = 4
    for m0 in range(0, MODES, tile):
        accs = [None] * (tile * VARS)
        for k in range(MODES):
            coefs = [coef_ref[v * MODES + k] for v in range(VARS)]
            for i in range(tile):
                entry = m_ref[0, (m0 + i) * MODES + k]
                for v in range(VARS):
                    term = entry * coefs[v]
                    old = accs[i * VARS + v]
                    accs[i * VARS + v] = term if old is None else old + term
        for i in range(tile):
            for v in range(VARS):
                f = v * MODES + m0 + i
                y_ref[pl.ds((f // 8) * 64 + f % 8, 8, stride=8), :] = accs[i * VARS + v]
    slots = 8 * LANES
    rows = []
    for fb in range(PADF // 8):
        rows.append(
            jnp.concatenate(
                [y_ref[(fb * 8 + g) * 8 : (fb * 8 + g) * 8 + 8, :] for g in range(8)], axis=1
            )
        )
    y = jnp.concatenate(rows, axis=0)
    high = y.astype(half).astype(single)
    both = jnp.concatenate([high, y - high], axis=0).astype(half)
    target = jnp.concatenate([target_ref[g : g + 1, :] for g in range(8)], axis=1)
    fold = target // BINS
    for a in range(folds):
        keep = jnp.where(fold == a, 1.0, 0.0).astype(half)
        lhs_ref[a * 2 * PADF : (a + 1) * 2 * PADF, :] = both * keep
    bins = lax.broadcasted_iota(jnp.int32, (256, slots), 0).astype(single).astype(half)
    within = target & (BINS - 1)
    parts = []
    for h in range(BINS // 256):
        wanted = (within - 256 * h).astype(single).astype(half)
        parts.append(jnp.where(bins == wanted, jnp.array(1, half), jnp.array(0, half)))
    acc_ref[...] += lax.dot_general(
        lhs_ref[...],
        jnp.concatenate(parts, axis=0),
        (((1,), (1,)), ((), ())),
        preferred_element_type=single,
    )

    @pl.when(turn == pl.num_programs(0) - 1)
    def _():
        minv = minv_ref[...]
        minv_h = minv.astype(half).astype(single)
        left = jnp.concatenate([minv_h, minv_h, minv - minv_h], axis=1).astype(half)
        scale = 1.0 / jac_ref[...]
        for a in range(folds):
            base = a * 2 * PADF
            rhs = acc_ref[base : base + PADF, :] + acc_ref[base + PADF : base + 2 * PADF, :]
            rhs_h = rhs.astype(half).astype(single)
            right = jnp.concatenate([rhs_h, rhs - rhs_h, rhs_h], axis=0).astype(half)
            done = jnp.dot(left, right, preferred_element_type=single)
            done = done * scale[:, a * BINS : (a + 1) * BINS]
            for j in range(BINS // LANES):
                out_ref[a * BINS + j * LANES : a * BINS + (j + 1) * LANES, :] = done[
                    :, j * LANES : (j + 1) * LANES
                ].T


def project(received, matrix, target, minv, jac):
    blocks = matrix.shape[0]
    count = jac.shape[1]
    folds = count // BINS
    return pl.pallas_call(
        project_kernel,
        grid=(blocks,),
        out_shape=jax.ShapeDtypeStruct((count, LANES), jnp.float32),
        in_specs=[
            pl.BlockSpec(memory_space=pltpu.VMEM),
            pl.BlockSpec((1, MODES * MODES, 8, LANES), lambda i: (i, 0, 0, 0)),
            pl.BlockSpec((8, LANES), lambda i: (i, 0)),
            pl.BlockSpec((LANES, PADF), lambda i: (0, 0)),
            pl.BlockSpec((1, count), lambda i: (0, 0)),
        ],
        out_specs=pl.BlockSpec((count, LANES), lambda i: (0, 0)),
        scratch_shapes=[
            pltpu.VMEM((ROWS, 8, LANES), jnp.float32),
            pltpu.VMEM((PADF * 8, LANES), jnp.float32),
            pltpu.VMEM((folds * 2 * PADF, 8 * LANES), jnp.bfloat16),
            pltpu.VMEM((folds * 2 * PADF, BINS), jnp.float32),
        ],
        compiler_params=pltpu.CompilerParams(vmem_limit_bytes=44 << 20),
        name="project",
    )(received, matrix, target, minv, jac)


def local(old_coef, old_index, pair_count, new_index, old_points, new_points, weights, jacobian,
          minv_ref, send_order):
    axes = ("dom", "sub")
    devices = lax.axis_size(axes)
    myself = lax.axis_index(axes)
    counts = lax.dynamic_slice_in_dim(pair_count, myself, 1, 0)[0]
    outgoing = gather(old_coef, old_index, counts)
    outgoing = outgoing.reshape(devices, HALF // 2, 2, LANES)
    received = lax.all_to_all(outgoing, axes, split_axis=0, concat_axis=0, tiled=True)
    received = received.reshape(devices * HALF, LANES)
    matrix = moment_matrix(old_points, new_points, weights)
    target, jac, minv = index_tables(send_order[0], new_index, jacobian, minv_ref)
    leaving = project(received, matrix, target, minv, jac.reshape(1, -1))
    leaving = leaving.reshape(devices, -1, LANES)
    arrived = lax.all_to_all(leaving, axes, split_axis=0, concat_axis=0, tiled=True)
    return arrived.reshape(-1, LANES)[:, :ROWS].T


def solution(mesh):
    placed = (
        P(None, ("dom", "sub")),
        P(("dom", "sub")),
        P(),
        P(("dom", "sub")),
        P(None, ("dom", "sub")),
        P(None, ("dom", "sub")),
        P(("dom", "sub")),
        P(("dom", "sub")),
        P(),
        P(("dom", "sub"), None),
    )
    return jax.shard_map(
        local, mesh=mesh, in_specs=placed, out_specs=P(None, ("dom", "sub")), check_vma=False
    )
```

```python
import functools
import jax
import jax.numpy as jnp
from jax import lax
from jax.experimental import pallas as pl
from jax.experimental.pallas import tpu as pltpu
from jax.sharding import PartitionSpec as P

VARS = 5
MODES = 20
ROWS = 100
HALF = 50
QUAD = 24
CAP = 64
LANES = 128


def gather_kernel(subs, idx_ref, cnt_ref, coef_ref, out_ref, tab_ref, buf_ref):
    part = pl.program_id(0)
    myself = lax.axis_index("dom") * subs + lax.axis_index("sub")
    width = coef_ref.shape[1]
    pairs = buf_ref.shape[0] // LANES
    lane = lax.broadcasted_iota(jnp.int32, (1, LANES), 1)
    low = lane < 64

    @pl.when(part == 0)
    def _():
        pad = jnp.zeros((64 - HALF, LANES), jnp.float32)

        def build(j, carry):
            start = pl.multiple_of(j * LANES, LANES)
            block = coef_ref[:, pl.ds(start, LANES)]
            wide = jnp.concatenate([block[:HALF], pad, block[HALF:], pad], axis=0)
            tab_ref[pl.ds(start, LANES), :] = wide.T
            return carry

        lax.fori_loop(0, width // LANES, build, 0, unroll=4)

    def fetch(t, carry):
        base = pl.multiple_of(t * LANES, LANES)
        first = (part * pairs + t) * LANES
        for j in range(LANES):
            buf_ref[pl.ds(base + j, 1), :] = tab_ref[pl.ds(idx_ref[first + j], 1), :]
        return carry

    lax.fori_loop(0, pairs, fetch, 0)

    turned = [buf_ref[u * LANES : (u + 1) * LANES, :].T for u in range(pairs)]
    for u in range(pairs):
        pair = part * pairs + u
        limit = jnp.where(low, cnt_ref[myself, 2 * pair], cnt_ref[myself, 2 * pair + 1] + 64)
        live = lane < limit
        first = jnp.where(live, turned[u][:HALF], 0.0)
        second = jnp.where(live, turned[u][64 : 64 + HALF], 0.0)
        out_ref[u * ROWS : u * ROWS + HALF, :] = jnp.where(low, first, pltpu.roll(second, 64, 1))
        out_ref[u * ROWS + HALF : (u + 1) * ROWS, :] = jnp.where(
            low, pltpu.roll(first, 64, 1), second
        )


def gather(old_coef, old_index, pair_count, subs, steps=4):
    slots = old_index.shape[0]
    rows, width = old_coef.shape
    total = slots // CAP * HALF
    return pl.pallas_call(
        functools.partial(gather_kernel, subs),
        grid=(steps,),
        out_shape=jax.ShapeDtypeStruct((total, LANES), jnp.float32),
        in_specs=[
            pl.BlockSpec(memory_space=pltpu.SMEM),
            pl.BlockSpec(memory_space=pltpu.SMEM),
            pl.BlockSpec((rows, width), lambda i: (0, 0), pipeline_mode=pl.Buffered(1)),
        ],
        out_specs=pl.BlockSpec((total // steps, LANES), lambda i: (i, 0)),
        scratch_shapes=[
            pltpu.VMEM((width, LANES), jnp.float32),
            pltpu.VMEM((slots // steps, LANES), jnp.float32),
        ],
        name="gather",
    )(old_index, pair_count, old_coef)


def monomials(first, second, third):
    unit = None
    fp = [unit, first, first * first]
    fp.append(fp[2] * first)
    sp = [unit, second, second * second]
    sp.append(sp[2] * second)
    tp = [unit, third, third * third]
    tp.append(tp[2] * third)
    rows = []
    for degree in range(4):
        for a in range(degree, -1, -1):
            for b in range(degree - a, -1, -1):
                out = None
                for term in (fp[a], sp[b], tp[degree - a - b]):
                    if term is not None:
                        out = term if out is None else out * term
                rows.append(out)
    return rows


def moment_kernel(old_ref, new_ref, w_ref, out_ref, po_ref, pn_ref):
    def basis(q, carry):
        weight = w_ref[q]
        old = monomials(*[old_ref[a, q] for a in range(3)])
        new = monomials(*[new_ref[a, q] for a in range(3)])
        for k in range(1, MODES):
            pn_ref[q, k] = new[k] * weight
            if k > 3:
                po_ref[q, k] = old[k]
        return carry

    lax.fori_loop(0, QUAD, basis, 0, unroll=2)
    tile = 5
    zero = jnp.zeros((8, LANES), jnp.float32)

    def weighted(q, m):
        return w_ref[q] if m == 0 else pn_ref[q, m]

    def plain(q, k):
        if k == 0:
            return None
        return old_ref[k - 1, q] if k < 4 else po_ref[q, k]

    for m0 in range(0, MODES, tile):
        for k0 in range(0, MODES, tile):

            def add(q, accs):
                left = [weighted(q, m0 + i) for i in range(tile)]
                right = [plain(q, k0 + j) for j in range(tile)]
                return tuple(
                    accs[i * tile + j] + (left[i] if right[j] is None else left[i] * right[j])
                    for i in range(tile)
                    for j in range(tile)
                )

            accs = lax.fori_loop(0, QUAD, add, (zero,) * (tile * tile), unroll=12)
            for i in range(tile):
                for j in range(tile):
                    out_ref[0, (m0 + i) * MODES + k0 + j] = accs[i * tile + j]


def moment_matrix(old_points, new_points, weights):
    groups = weights.shape[0] // QUAD // LANES
    blocks = groups // 8
    shape = (3, QUAD, groups, LANES)
    return pl.pallas_call(
        moment_kernel,
        grid=(blocks,),
        out_shape=jax.ShapeDtypeStruct((blocks, MODES * MODES, 8, LANES), jnp.float32),
        in_specs=[
            pl.BlockSpec((3, QUAD, 8, LANES), lambda i: (0, 0, i, 0)),
            pl.BlockSpec((3, QUAD, 8, LANES), lambda i: (0, 0, i, 0)),
            pl.BlockSpec((QUAD, 8, LANES), lambda i: (0, i, 0)),
        ],
        out_specs=pl.BlockSpec((1, MODES * MODES, 8, LANES), lambda i: (i, 0, 0, 0)),
        scratch_shapes=[
            pltpu.VMEM((QUAD, MODES, 8, LANES), jnp.float32),
            pltpu.VMEM((QUAD, MODES, 8, LANES), jnp.float32),
        ],
        cost_estimate=pl.CostEstimate(
            flops=int(20e-6 * 1.1e15), bytes_accessed=40 * 2**20, transcendentals=0
        ),
        name="moment_matrix",
    )(old_points.reshape(shape), new_points.reshape(shape), weights.reshape(shape[1:]))


def index_kernel(order_s, index_ref, jac_ref, order_ref, minv_ref, target_ref, jacp_ref, wide_ref):
    wide_ref[...] = jnp.zeros_like(wide_ref)
    for v in range(VARS):
        wide_ref[v * MODES : (v + 1) * MODES, v * MODES : (v + 1) * MODES] = minv_ref[...]
    rows = jac_ref.shape[0]
    place = lax.broadcasted_iota(jnp.int32, (rows, LANES), 0) * LANES + lax.broadcasted_iota(
        jnp.int32, (rows, LANES), 1
    )

    def invert(p, inverse):
        return jnp.where(place == order_s[p], p, inverse)

    inverse = lax.fori_loop(
        0, rows * LANES, invert, jnp.zeros((rows, LANES), jnp.int32), unroll=8
    )

    def look(table, index):
        low = index & (LANES - 1)
        high = index >> 7
        found = jnp.zeros(index.shape, table.dtype)
        for r in range(rows):
            row = jnp.broadcast_to(table[r : r + 1], index.shape)
            found = jnp.where(high == r, jnp.take_along_axis(row, low, axis=1), found)
        return found

    for g in range(index_ref.shape[0] // 8):
        target_ref[8 * g : 8 * g + 8, :] = look(inverse, index_ref[8 * g : 8 * g + 8, :])
    jac = jac_ref[...]
    for g in range(rows // 8):
        jacp_ref[8 * g : 8 * g + 8, :] = look(jac, order_ref[8 * g : 8 * g + 8, :])


def index_tables(order, new_index, jacobian, minv):
    slots = new_index.shape[0]
    count = order.shape[0]
    vm = pl.BlockSpec(memory_space=pltpu.VMEM)
    return pl.pallas_call(
        index_kernel,
        out_shape=(
            jax.ShapeDtypeStruct((slots // LANES, LANES), jnp.int32),
            jax.ShapeDtypeStruct((count // LANES, LANES), jnp.float32),
            jax.ShapeDtypeStruct((LANES, PADF), jnp.float32),
        ),
        in_specs=[pl.BlockSpec(memory_space=pltpu.SMEM), vm, vm, vm, vm],
        out_specs=(vm, vm, vm),
        cost_estimate=pl.CostEstimate(
            flops=int(4e-6 * 1.1e15), bytes_accessed=8 * 2**20, transcendentals=0
        ),
        compiler_params=pltpu.CompilerParams(vmem_limit_bytes=8 << 20),
        name="index_tables",
    )(
        order,
        new_index.reshape(-1, LANES),
        jacobian.reshape(-1, LANES),
        order.reshape(-1, LANES),
        minv,
    )


PADF = 104
BINS = 512


def project_kernel(
    recv_ref, m_ref, target_ref, minv_ref, jac_ref, out_ref, coef_ref, y_ref, lhs_ref, acc_ref
):
    turn = pl.program_id(0)
    folds = acc_ref.shape[0] // (2 * PADF)
    half = jnp.bfloat16
    single = jnp.float32

    @pl.when(turn == 0)
    def _():
        acc_ref[...] = jnp.zeros_like(acc_ref)
        y_ref[...] = jnp.zeros_like(y_ref)

    low = lax.broadcasted_iota(jnp.int32, (8, LANES), 1) < 64
    first = pl.multiple_of(turn * (8 * ROWS), 8)
    for r in range(HALF):
        even = recv_ref[pl.ds(first + r, 8, stride=ROWS), :]
        odd = recv_ref[pl.ds(first + HALF + r, 8, stride=ROWS), :]
        coef_ref[r] = jnp.where(low, even, pltpu.roll(odd, 64, 1))
        coef_ref[r + HALF] = jnp.where(low, pltpu.roll(even, 64, 1), odd)
    tile = 4
    for m0 in range(0, MODES, tile):
        accs = [None] * (tile * VARS)
        for k in range(MODES):
            coefs = [coef_ref[v * MODES + k] for v in range(VARS)]
            for i in range(tile):
                entry = m_ref[0, (m0 + i) * MODES + k]
                for v in range(VARS):
                    term = entry * coefs[v]
                    old = accs[i * VARS + v]
                    accs[i * VARS + v] = term if old is None else old + term
        for i in range(tile):
            for v in range(VARS):
                f = v * MODES + m0 + i
                y_ref[pl.ds((f // 8) * 64 + f % 8, 8, stride=8), :] = accs[i * VARS + v]
    slots = 8 * LANES
    rows = []
    for fb in range(PADF // 8):
        rows.append(
            jnp.concatenate(
                [y_ref[(fb * 8 + g) * 8 : (fb * 8 + g) * 8 + 8, :] for g in range(8)], axis=1
            )
        )
    y = jnp.concatenate(rows, axis=0)
    high = y.astype(half).astype(single)
    both = jnp.concatenate([high, y - high], axis=0).astype(half)
    target = jnp.concatenate([target_ref[g : g + 1, :] for g in range(8)], axis=1)
    fold = target // BINS
    for a in range(folds):
        keep = jnp.where(fold == a, 1.0, 0.0).astype(half)
        lhs_ref[a * 2 * PADF : (a + 1) * 2 * PADF, :] = both * keep
    bins = lax.broadcasted_iota(jnp.int32, (256, slots), 0).astype(single).astype(half)
    within = target & (BINS - 1)
    parts = []
    for h in range(BINS // 256):
        wanted = (within - 256 * h).astype(single).astype(half)
        parts.append(jnp.where(bins == wanted, jnp.array(1, half), jnp.array(0, half)))
    acc_ref[...] += lax.dot_general(
        lhs_ref[...],
        jnp.concatenate(parts, axis=0),
        (((1,), (1,)), ((), ())),
        preferred_element_type=single,
    )

    @pl.when(turn == pl.num_programs(0) - 1)
    def _():
        minv = minv_ref[...]
        minv_h = minv.astype(half).astype(single)
        left = jnp.concatenate([minv_h, minv_h, minv - minv_h], axis=1).astype(half)
        scale = 1.0 / jac_ref[...]
        for a in range(folds):
            base = a * 2 * PADF
            rhs = acc_ref[base : base + PADF, :] + acc_ref[base + PADF : base + 2 * PADF, :]
            rhs_h = rhs.astype(half).astype(single)
            right = jnp.concatenate([rhs_h, rhs - rhs_h, rhs_h], axis=0).astype(half)
            done = jnp.dot(left, right, preferred_element_type=single)
            done = done * scale[:, a * BINS : (a + 1) * BINS]
            for j in range(BINS // LANES):
                out_ref[a * BINS + j * LANES : a * BINS + (j + 1) * LANES, :] = done[
                    :, j * LANES : (j + 1) * LANES
                ].T


def project(received, matrix, target, minv, jac):
    blocks = matrix.shape[0]
    count = jac.shape[1]
    folds = count // BINS
    return pl.pallas_call(
        project_kernel,
        grid=(blocks,),
        out_shape=jax.ShapeDtypeStruct((count, LANES), jnp.float32),
        in_specs=[
            pl.BlockSpec(memory_space=pltpu.VMEM),
            pl.BlockSpec((1, MODES * MODES, 8, LANES), lambda i: (i, 0, 0, 0)),
            pl.BlockSpec((8, LANES), lambda i: (i, 0)),
            pl.BlockSpec((LANES, PADF), lambda i: (0, 0)),
            pl.BlockSpec((1, count), lambda i: (0, 0)),
        ],
        out_specs=pl.BlockSpec((count, LANES), lambda i: (0, 0)),
        scratch_shapes=[
            pltpu.VMEM((ROWS, 8, LANES), jnp.float32),
            pltpu.VMEM((PADF * 8, LANES), jnp.float32),
            pltpu.VMEM((folds * 2 * PADF, 8 * LANES), jnp.bfloat16),
            pltpu.VMEM((folds * 2 * PADF, BINS), jnp.float32),
        ],
        compiler_params=pltpu.CompilerParams(vmem_limit_bytes=44 << 20),
        name="project",
    )(received, matrix, target, minv, jac)


def local(old_coef, old_index, pair_count, new_index, old_points, new_points, weights, jacobian,
          minv_ref, send_order):
    axes = ("dom", "sub")
    devices = lax.axis_size(axes)
    outgoing = gather(old_coef, old_index, pair_count, lax.axis_size("sub"))
    outgoing = outgoing.reshape(devices, HALF // 2, 2, LANES)
    received = lax.all_to_all(outgoing, axes, split_axis=0, concat_axis=0, tiled=True)
    received = received.reshape(devices * HALF, LANES)
    target, jac, minv = index_tables(send_order[0], new_index, jacobian, minv_ref)
    old_points, new_points, target = lax.optimization_barrier((old_points, new_points, target))
    matrix = moment_matrix(old_points, new_points, weights)
    leaving = project(received, matrix, target, minv, jac.reshape(1, -1))
    leaving = leaving.reshape(devices, -1, LANES)
    arrived = lax.all_to_all(leaving, axes, split_axis=0, concat_axis=0, tiled=True)
    return arrived.reshape(-1, LANES)[:, :ROWS].T


def solution(mesh):
    placed = (
        P(None, ("dom", "sub")),
        P(("dom", "sub")),
        P(),
        P(("dom", "sub")),
        P(None, ("dom", "sub")),
        P(None, ("dom", "sub")),
        P(("dom", "sub")),
        P(("dom", "sub")),
        P(),
        P(("dom", "sub"), None),
    )
    return jax.shard_map(
        local, mesh=mesh, in_specs=placed, out_specs=P(None, ("dom", "sub")), check_vma=False
    )
```

```python
import functools
import jax
import jax.numpy as jnp
from jax import lax
from jax.experimental import pallas as pl
from jax.experimental.pallas import tpu as pltpu
from jax.sharding import PartitionSpec as P

VARS = 5
MODES = 20
ROWS = 100
HALF = 50
QUAD = 24
CAP = 64
LANES = 128


def gather_kernel(
    subs, idx_hbm, cnt_hbm, coef_hbm, out_ref, tab_ref, buf_ref, coef_ref, idx_ref, cnt_ref, sems
):
    part = pl.program_id(0)
    rank = lax.axis_index("dom") * subs + lax.axis_index("sub")
    myself = rank % 8
    width = coef_ref.shape[1]
    pairs = buf_ref.shape[0] // LANES
    lane = lax.broadcasted_iota(jnp.int32, (1, LANES), 1)
    low = lane < 64

    @pl.when(part == 0)
    def _():
        cuts = 4
        span = width // cuts
        wide = [
            pltpu.make_async_copy(
                coef_hbm.at[:, pl.ds(c * span, span)],
                coef_ref.at[:, pl.ds(c * span, span)],
                sems.at[c],
            )
            for c in range(cuts)
        ]
        start = pl.multiple_of(rank - myself, 8)
        small = [
            pltpu.make_async_copy(idx_hbm, idx_ref, sems.at[cuts]),
            pltpu.make_async_copy(cnt_hbm.at[pl.ds(start, 8), :], cnt_ref, sems.at[cuts + 1]),
        ]
        for copy in wide[:1] + small + wide[1:]:
            copy.start()
        pad = jnp.zeros((64 - HALF, LANES), jnp.float32)

        def build(j, carry):
            start = pl.multiple_of(j * LANES, LANES)
            block = coef_ref[:, pl.ds(start, LANES)]
            wide = jnp.concatenate([block[:HALF], pad, block[HALF:], pad], axis=0)
            tab_ref[pl.ds(start, LANES), :] = wide.T
            return carry

        for c in range(cuts):
            wide[c].wait()
            lax.fori_loop(c * (span // LANES), (c + 1) * (span // LANES), build, 0, unroll=4)
        for copy in small:
            copy.wait()

    def fetch(t, carry):
        base = pl.multiple_of(t * LANES, LANES)
        first = (part * pairs + t) * LANES
        for j in range(LANES):
            buf_ref[pl.ds(base + j, 1), :] = tab_ref[pl.ds(idx_ref[first + j], 1), :]
        return carry

    lax.fori_loop(0, pairs, fetch, 0)

    turned = [buf_ref[u * LANES : (u + 1) * LANES, :].T for u in range(pairs)]
    for u in range(pairs):
        pair = part * pairs + u
        limit = jnp.where(low, cnt_ref[myself, 2 * pair], cnt_ref[myself, 2 * pair + 1] + 64)
        live = lane < limit
        first = jnp.where(live, turned[u][:HALF], 0.0)
        second = jnp.where(live, turned[u][64 : 64 + HALF], 0.0)
        out_ref[u * ROWS : u * ROWS + HALF, :] = jnp.where(low, first, pltpu.roll(second, 64, 1))
        out_ref[u * ROWS + HALF : (u + 1) * ROWS, :] = jnp.where(
            low, pltpu.roll(first, 64, 1), second
        )


def gather(old_coef, old_index, pair_count, subs, steps=4):
    slots = old_index.shape[0]
    rows, width = old_coef.shape
    total = slots // CAP * HALF
    return pl.pallas_call(
        functools.partial(gather_kernel, subs),
        grid=(steps,),
        out_shape=jax.ShapeDtypeStruct((total, LANES), jnp.float32),
        in_specs=[pl.BlockSpec(memory_space=pl.ANY)] * 3,
        out_specs=pl.BlockSpec((total // steps, LANES), lambda i: (i, 0)),
        scratch_shapes=[
            pltpu.VMEM((width, LANES), jnp.float32),
            pltpu.VMEM((slots // steps, LANES), jnp.float32),
            pltpu.VMEM((rows, width), jnp.float32),
            pltpu.SMEM((slots,), jnp.int32),
            pltpu.SMEM((8, pair_count.shape[1]), jnp.int32),
            pltpu.SemaphoreType.DMA((6,)),
        ],
        name="gather",
    )(old_index, pair_count, old_coef)


def monomials(first, second, third):
    unit = None
    fp = [unit, first, first * first]
    fp.append(fp[2] * first)
    sp = [unit, second, second * second]
    sp.append(sp[2] * second)
    tp = [unit, third, third * third]
    tp.append(tp[2] * third)
    rows = []
    for degree in range(4):
        for a in range(degree, -1, -1):
            for b in range(degree - a, -1, -1):
                out = None
                for term in (fp[a], sp[b], tp[degree - a - b]):
                    if term is not None:
                        out = term if out is None else out * term
                rows.append(out)
    return rows


def moment_kernel(old_ref, new_ref, w_ref, out_ref, po_ref, pn_ref):
    def basis(q, carry):
        weight = w_ref[q]
        old = monomials(*[old_ref[a, q] for a in range(3)])
        new = monomials(*[new_ref[a, q] for a in range(3)])
        for k in range(1, MODES):
            pn_ref[q, k] = new[k] * weight
            if k > 3:
                po_ref[q, k] = old[k]
        return carry

    lax.fori_loop(0, QUAD, basis, 0, unroll=2)
    tile = 5
    zero = jnp.zeros((8, LANES), jnp.float32)

    def weighted(q, m):
        return w_ref[q] if m == 0 else pn_ref[q, m]

    def plain(q, k):
        if k == 0:
            return None
        return old_ref[k - 1, q] if k < 4 else po_ref[q, k]

    for m0 in range(0, MODES, tile):
        for k0 in range(0, MODES, tile):

            def add(q, accs):
                left = [weighted(q, m0 + i) for i in range(tile)]
                right = [plain(q, k0 + j) for j in range(tile)]
                return tuple(
                    accs[i * tile + j] + (left[i] if right[j] is None else left[i] * right[j])
                    for i in range(tile)
                    for j in range(tile)
                )

            accs = lax.fori_loop(0, QUAD, add, (zero,) * (tile * tile), unroll=12)
            for i in range(tile):
                for j in range(tile):
                    out_ref[0, (m0 + i) * MODES + k0 + j] = accs[i * tile + j]


def moment_matrix(old_points, new_points, weights):
    groups = weights.shape[0] // QUAD // LANES
    blocks = groups // 8
    shape = (3, QUAD, groups, LANES)
    return pl.pallas_call(
        moment_kernel,
        grid=(blocks,),
        out_shape=jax.ShapeDtypeStruct((blocks, MODES * MODES, 8, LANES), jnp.float32),
        in_specs=[
            pl.BlockSpec((3, QUAD, 8, LANES), lambda i: (0, 0, i, 0)),
            pl.BlockSpec((3, QUAD, 8, LANES), lambda i: (0, 0, i, 0)),
            pl.BlockSpec((QUAD, 8, LANES), lambda i: (0, i, 0)),
        ],
        out_specs=pl.BlockSpec((1, MODES * MODES, 8, LANES), lambda i: (i, 0, 0, 0)),
        scratch_shapes=[
            pltpu.VMEM((QUAD, MODES, 8, LANES), jnp.float32),
            pltpu.VMEM((QUAD, MODES, 8, LANES), jnp.float32),
        ],
        cost_estimate=pl.CostEstimate(
            flops=int(20e-6 * 1.1e15), bytes_accessed=40 * 2**20, transcendentals=0
        ),
        name="moment_matrix",
    )(old_points.reshape(shape), new_points.reshape(shape), weights.reshape(shape[1:]))


def index_kernel(order_s, index_ref, jac_ref, order_ref, minv_ref, target_ref, jacp_ref, wide_ref):
    wide_ref[...] = jnp.zeros_like(wide_ref)
    for v in range(VARS):
        wide_ref[v * MODES : (v + 1) * MODES, v * MODES : (v + 1) * MODES] = minv_ref[...]
    rows = jac_ref.shape[0]
    place = lax.broadcasted_iota(jnp.int32, (rows, LANES), 0) * LANES + lax.broadcasted_iota(
        jnp.int32, (rows, LANES), 1
    )

    def invert(p, inverse):
        return jnp.where(place == order_s[p], p, inverse)

    inverse = lax.fori_loop(
        0, rows * LANES, invert, jnp.zeros((rows, LANES), jnp.int32), unroll=8
    )

    def look(table, index):
        low = index & (LANES - 1)
        high = index >> 7
        found = jnp.zeros(index.shape, table.dtype)
        for r in range(rows):
            row = jnp.broadcast_to(table[r : r + 1], index.shape)
            found = jnp.where(high == r, jnp.take_along_axis(row, low, axis=1), found)
        return found

    for g in range(index_ref.shape[0] // 8):
        target_ref[8 * g : 8 * g + 8, :] = look(inverse, index_ref[8 * g : 8 * g + 8, :])
    jac = jac_ref[...]
    for g in range(rows // 8):
        jacp_ref[8 * g : 8 * g + 8, :] = look(jac, order_ref[8 * g : 8 * g + 8, :])


def index_tables(order, new_index, jacobian, minv):
    slots = new_index.shape[0]
    count = order.shape[0]
    vm = pl.BlockSpec(memory_space=pltpu.VMEM)
    return pl.pallas_call(
        index_kernel,
        out_shape=(
            jax.ShapeDtypeStruct((slots // LANES, LANES), jnp.int32),
            jax.ShapeDtypeStruct((count // LANES, LANES), jnp.float32),
            jax.ShapeDtypeStruct((LANES, PADF), jnp.float32),
        ),
        in_specs=[pl.BlockSpec(memory_space=pltpu.SMEM), vm, vm, vm, vm],
        out_specs=(vm, vm, vm),
        cost_estimate=pl.CostEstimate(
            flops=int(4e-6 * 1.1e15), bytes_accessed=8 * 2**20, transcendentals=0
        ),
        compiler_params=pltpu.CompilerParams(vmem_limit_bytes=8 << 20),
        name="index_tables",
    )(
        order,
        new_index.reshape(-1, LANES),
        jacobian.reshape(-1, LANES),
        order.reshape(-1, LANES),
        minv,
    )


PADF = 104
BINS = 512


def project_kernel(
    recv_ref, m_ref, target_ref, minv_ref, jac_ref, out_ref, coef_ref, y_ref, lhs_ref, acc_ref
):
    turn = pl.program_id(0)
    folds = acc_ref.shape[0] // (2 * PADF)
    half = jnp.bfloat16
    single = jnp.float32

    @pl.when(turn == 0)
    def _():
        acc_ref[...] = jnp.zeros_like(acc_ref)
        y_ref[...] = jnp.zeros_like(y_ref)

    low = lax.broadcasted_iota(jnp.int32, (8, LANES), 1) < 64
    first = pl.multiple_of(turn * (8 * ROWS), 8)
    for r in range(HALF):
        even = recv_ref[pl.ds(first + r, 8, stride=ROWS), :]
        odd = recv_ref[pl.ds(first + HALF + r, 8, stride=ROWS), :]
        coef_ref[r] = jnp.where(low, even, pltpu.roll(odd, 64, 1))
        coef_ref[r + HALF] = jnp.where(low, pltpu.roll(even, 64, 1), odd)
    tile = 4
    for m0 in range(0, MODES, tile):
        accs = [None] * (tile * VARS)
        for k in range(MODES):
            coefs = [coef_ref[v * MODES + k] for v in range(VARS)]
            for i in range(tile):
                entry = m_ref[0, (m0 + i) * MODES + k]
                for v in range(VARS):
                    term = entry * coefs[v]
                    old = accs[i * VARS + v]
                    accs[i * VARS + v] = term if old is None else old + term
        for i in range(tile):
            for v in range(VARS):
                f = v * MODES + m0 + i
                y_ref[pl.ds((f // 8) * 64 + f % 8, 8, stride=8), :] = accs[i * VARS + v]
    slots = 8 * LANES
    rows = []
    for fb in range(PADF // 8):
        rows.append(
            jnp.concatenate(
                [y_ref[(fb * 8 + g) * 8 : (fb * 8 + g) * 8 + 8, :] for g in range(8)], axis=1
            )
        )
    y = jnp.concatenate(rows, axis=0)
    high = y.astype(half).astype(single)
    both = jnp.concatenate([high, y - high], axis=0).astype(half)
    target = jnp.concatenate([target_ref[g : g + 1, :] for g in range(8)], axis=1)
    fold = target // BINS
    for a in range(folds):
        keep = jnp.where(fold == a, 1.0, 0.0).astype(half)
        lhs_ref[a * 2 * PADF : (a + 1) * 2 * PADF, :] = both * keep
    bins = lax.broadcasted_iota(jnp.int32, (256, slots), 0).astype(single).astype(half)
    within = target & (BINS - 1)
    parts = []
    for h in range(BINS // 256):
        wanted = (within - 256 * h).astype(single).astype(half)
        parts.append(jnp.where(bins == wanted, jnp.array(1, half), jnp.array(0, half)))
    acc_ref[...] += lax.dot_general(
        lhs_ref[...],
        jnp.concatenate(parts, axis=0),
        (((1,), (1,)), ((), ())),
        preferred_element_type=single,
    )

    @pl.when(turn == pl.num_programs(0) - 1)
    def _():
        minv = minv_ref[...]
        minv_h = minv.astype(half).astype(single)
        left = jnp.concatenate([minv_h, minv_h, minv - minv_h], axis=1).astype(half)
        scale = 1.0 / jac_ref[...]
        for a in range(folds):
            base = a * 2 * PADF
            rhs = acc_ref[base : base + PADF, :] + acc_ref[base + PADF : base + 2 * PADF, :]
            rhs_h = rhs.astype(half).astype(single)
            right = jnp.concatenate([rhs_h, rhs - rhs_h, rhs_h], axis=0).astype(half)
            done = jnp.dot(left, right, preferred_element_type=single)
            done = done * scale[:, a * BINS : (a + 1) * BINS]
            for j in range(BINS // LANES):
                out_ref[a * BINS + j * LANES : a * BINS + (j + 1) * LANES, :] = done[
                    :, j * LANES : (j + 1) * LANES
                ].T


def project(received, matrix, target, minv, jac):
    blocks = matrix.shape[0]
    count = jac.shape[1]
    folds = count // BINS
    return pl.pallas_call(
        project_kernel,
        grid=(blocks,),
        out_shape=jax.ShapeDtypeStruct((count, LANES), jnp.float32),
        in_specs=[
            pl.BlockSpec(memory_space=pltpu.VMEM),
            pl.BlockSpec((1, MODES * MODES, 8, LANES), lambda i: (i, 0, 0, 0)),
            pl.BlockSpec((8, LANES), lambda i: (i, 0)),
            pl.BlockSpec((LANES, PADF), lambda i: (0, 0)),
            pl.BlockSpec((1, count), lambda i: (0, 0)),
        ],
        out_specs=pl.BlockSpec((count, LANES), lambda i: (0, 0)),
        scratch_shapes=[
            pltpu.VMEM((ROWS, 8, LANES), jnp.float32),
            pltpu.VMEM((PADF * 8, LANES), jnp.float32),
            pltpu.VMEM((folds * 2 * PADF, 8 * LANES), jnp.bfloat16),
            pltpu.VMEM((folds * 2 * PADF, BINS), jnp.float32),
        ],
        compiler_params=pltpu.CompilerParams(vmem_limit_bytes=44 << 20),
        name="project",
    )(received, matrix, target, minv, jac)


def local(old_coef, old_index, pair_count, new_index, old_points, new_points, weights, jacobian,
          minv_ref, send_order):
    axes = ("dom", "sub")
    devices = lax.axis_size(axes)
    outgoing = gather(old_coef, old_index, pair_count, lax.axis_size("sub"))
    outgoing = outgoing.reshape(devices, HALF // 2, 2, LANES)
    received = lax.all_to_all(outgoing, axes, split_axis=0, concat_axis=0, tiled=True)
    received = received.reshape(devices * HALF, LANES)
    target, jac, minv = index_tables(send_order[0], new_index, jacobian, minv_ref)
    old_points, new_points, target = lax.optimization_barrier((old_points, new_points, target))
    matrix = moment_matrix(old_points, new_points, weights)
    leaving = project(received, matrix, target, minv, jac.reshape(1, -1))
    leaving = leaving.reshape(devices, -1, LANES)
    arrived = lax.all_to_all(leaving, axes, split_axis=0, concat_axis=0, tiled=True)
    return arrived.reshape(-1, LANES)[:, :ROWS].T


def solution(mesh):
    placed = (
        P(None, ("dom", "sub")),
        P(("dom", "sub")),
        P(),
        P(("dom", "sub")),
        P(None, ("dom", "sub")),
        P(None, ("dom", "sub")),
        P(("dom", "sub")),
        P(("dom", "sub")),
        P(),
        P(("dom", "sub"), None),
    )
    return jax.shard_map(
        local, mesh=mesh, in_specs=placed, out_specs=P(None, ("dom", "sub")), check_vma=False
    )
```

```python
import functools
import jax
import jax.numpy as jnp
from jax import lax
from jax.experimental import pallas as pl
from jax.experimental.pallas import tpu as pltpu
from jax.sharding import PartitionSpec as P

VARS = 5
MODES = 20
ROWS = 100
HALF = 50
QUAD = 24
CAP = 64
LANES = 128


def gather_kernel(
    subs, idx_hbm, cnt_hbm, coef_hbm, out_ref, tab_ref, buf_ref, coef_ref, idx_ref, cnt_ref, sems
):
    part = pl.program_id(0)
    rank = lax.axis_index("dom") * subs + lax.axis_index("sub")
    myself = rank % 8
    width = coef_ref.shape[1]
    pairs = buf_ref.shape[0] // LANES
    lane = lax.broadcasted_iota(jnp.int32, (1, LANES), 1)
    low = lane < 64

    @pl.when(part == 0)
    def _():
        cuts = 4
        span = width // cuts
        wide = [
            pltpu.make_async_copy(
                coef_hbm.at[:, pl.ds(c * span, span)],
                coef_ref.at[:, pl.ds(c * span, span)],
                sems.at[c],
            )
            for c in range(cuts)
        ]
        start = pl.multiple_of(rank - myself, 8)
        small = [
            pltpu.make_async_copy(idx_hbm, idx_ref, sems.at[cuts]),
            pltpu.make_async_copy(cnt_hbm.at[pl.ds(start, 8), :], cnt_ref, sems.at[cuts + 1]),
        ]
        for copy in wide[:1] + small + wide[1:]:
            copy.start()
        pad = jnp.zeros((64 - HALF, LANES), jnp.float32)

        def build(j, carry):
            start = pl.multiple_of(j * LANES, LANES)
            block = coef_ref[:, pl.ds(start, LANES)]
            wide = jnp.concatenate([block[:HALF], pad, block[HALF:], pad], axis=0)
            tab_ref[pl.ds(start, LANES), :] = wide.T
            return carry

        for c in range(cuts):
            wide[c].wait()
            lax.fori_loop(c * (span // LANES), (c + 1) * (span // LANES), build, 0, unroll=4)
        for copy in small:
            copy.wait()

    def fetch(t, carry):
        base = pl.multiple_of(t * LANES, LANES)
        first = (part * pairs + t) * LANES
        for j in range(LANES):
            buf_ref[pl.ds(base + j, 1), :] = tab_ref[pl.ds(idx_ref[first + j], 1), :]
        return carry

    lax.fori_loop(0, pairs, fetch, 0)

    turned = [buf_ref[u * LANES : (u + 1) * LANES, :].T for u in range(pairs)]
    for u in range(pairs):
        pair = part * pairs + u
        limit = jnp.where(low, cnt_ref[myself, 2 * pair], cnt_ref[myself, 2 * pair + 1] + 64)
        live = lane < limit
        first = jnp.where(live, turned[u][:HALF], 0.0)
        second = jnp.where(live, turned[u][64 : 64 + HALF], 0.0)
        out_ref[u * ROWS : u * ROWS + HALF, :] = jnp.where(low, first, pltpu.roll(second, 64, 1))
        out_ref[u * ROWS + HALF : (u + 1) * ROWS, :] = jnp.where(
            low, pltpu.roll(first, 64, 1), second
        )


def gather(old_coef, old_index, pair_count, subs, steps=4):
    slots = old_index.shape[0]
    rows, width = old_coef.shape
    total = slots // CAP * HALF
    return pl.pallas_call(
        functools.partial(gather_kernel, subs),
        grid=(steps,),
        out_shape=jax.ShapeDtypeStruct((total, LANES), jnp.float32),
        in_specs=[pl.BlockSpec(memory_space=pl.ANY)] * 3,
        out_specs=pl.BlockSpec((total // steps, LANES), lambda i: (i, 0)),
        scratch_shapes=[
            pltpu.VMEM((width, LANES), jnp.float32),
            pltpu.VMEM((slots // steps, LANES), jnp.float32),
            pltpu.VMEM((rows, width), jnp.float32),
            pltpu.SMEM((slots,), jnp.int32),
            pltpu.SMEM((8, pair_count.shape[1]), jnp.int32),
            pltpu.SemaphoreType.DMA((6,)),
        ],
        name="gather",
    )(old_index, pair_count, old_coef)


def monomials(first, second, third):
    unit = None
    fp = [unit, first, first * first]
    fp.append(fp[2] * first)
    sp = [unit, second, second * second]
    sp.append(sp[2] * second)
    tp = [unit, third, third * third]
    tp.append(tp[2] * third)
    rows = []
    for degree in range(4):
        for a in range(degree, -1, -1):
            for b in range(degree - a, -1, -1):
                out = None
                for term in (fp[a], sp[b], tp[degree - a - b]):
                    if term is not None:
                        out = term if out is None else out * term
                rows.append(out)
    return rows


def moment_kernel(old_ref, new_ref, w_ref, out_ref, po_ref, pn_ref):
    def basis(q, carry):
        weight = w_ref[q]
        old = monomials(*[old_ref[a, q] for a in range(3)])
        new = monomials(*[new_ref[a, q] for a in range(3)])
        for k in range(1, MODES):
            pn_ref[q, k] = new[k] * weight
            if k > 3:
                po_ref[q, k] = old[k]
        return carry

    lax.fori_loop(0, QUAD, basis, 0, unroll=2)
    tile = 5
    zero = jnp.zeros((8, LANES), jnp.float32)

    def weighted(q, m):
        return w_ref[q] if m == 0 else pn_ref[q, m]

    def plain(q, k):
        if k == 0:
            return None
        return old_ref[k - 1, q] if k < 4 else po_ref[q, k]

    for m0 in range(0, MODES, tile):
        for k0 in range(0, MODES, tile):

            def add(q, accs):
                left = [weighted(q, m0 + i) for i in range(tile)]
                right = [plain(q, k0 + j) for j in range(tile)]
                return tuple(
                    accs[i * tile + j] + (left[i] if right[j] is None else left[i] * right[j])
                    for i in range(tile)
                    for j in range(tile)
                )

            accs = lax.fori_loop(0, QUAD, add, (zero,) * (tile * tile), unroll=12)
            for i in range(tile):
                for j in range(tile):
                    out_ref[0, (m0 + i) * MODES + k0 + j] = accs[i * tile + j]


def moment_matrix(old_points, new_points, weights):
    groups = weights.shape[0] // QUAD // LANES
    blocks = groups // 8
    shape = (3, QUAD, groups, LANES)
    return pl.pallas_call(
        moment_kernel,
        grid=(blocks,),
        out_shape=jax.ShapeDtypeStruct((blocks, MODES * MODES, 8, LANES), jnp.float32),
        in_specs=[
            pl.BlockSpec((3, QUAD, 8, LANES), lambda i: (0, 0, i, 0)),
            pl.BlockSpec((3, QUAD, 8, LANES), lambda i: (0, 0, i, 0)),
            pl.BlockSpec((QUAD, 8, LANES), lambda i: (0, i, 0)),
        ],
        out_specs=pl.BlockSpec((1, MODES * MODES, 8, LANES), lambda i: (i, 0, 0, 0)),
        scratch_shapes=[
            pltpu.VMEM((QUAD, MODES, 8, LANES), jnp.float32),
            pltpu.VMEM((QUAD, MODES, 8, LANES), jnp.float32),
        ],
        cost_estimate=pl.CostEstimate(
            flops=int(20e-6 * 1.1e15), bytes_accessed=40 * 2**20, transcendentals=0
        ),
        name="moment_matrix",
    )(old_points.reshape(shape), new_points.reshape(shape), weights.reshape(shape[1:]))


def index_kernel(order_s, index_ref, jac_ref, order_ref, minv_ref, target_ref, jacp_ref, wide_ref):
    wide_ref[...] = jnp.zeros_like(wide_ref)
    span = MODES // 2
    for v in range(VARS):
        for h in range(2):
            start = h * PADH + v * span
            wide_ref[v * MODES : (v + 1) * MODES, start : start + span] = minv_ref[
                :, h * span : (h + 1) * span
            ]
    rows = jac_ref.shape[0]
    place = lax.broadcasted_iota(jnp.int32, (rows, LANES), 0) * LANES + lax.broadcasted_iota(
        jnp.int32, (rows, LANES), 1
    )

    def invert(p, inverse):
        return jnp.where(place == order_s[p], p, inverse)

    inverse = lax.fori_loop(
        0, rows * LANES, invert, jnp.zeros((rows, LANES), jnp.int32), unroll=8
    )

    def look(table, index):
        low = index & (LANES - 1)
        high = index >> 7
        found = jnp.zeros(index.shape, table.dtype)
        for r in range(rows):
            row = jnp.broadcast_to(table[r : r + 1], index.shape)
            found = jnp.where(high == r, jnp.take_along_axis(row, low, axis=1), found)
        return found

    for g in range(index_ref.shape[0] // 8):
        target_ref[8 * g : 8 * g + 8, :] = look(inverse, index_ref[8 * g : 8 * g + 8, :])
    jac = jac_ref[...]
    for g in range(rows // 8):
        jacp_ref[8 * g : 8 * g + 8, :] = look(jac, order_ref[8 * g : 8 * g + 8, :])


def index_tables(order, new_index, jacobian, minv):
    slots = new_index.shape[0]
    count = order.shape[0]
    vm = pl.BlockSpec(memory_space=pltpu.VMEM)
    return pl.pallas_call(
        index_kernel,
        out_shape=(
            jax.ShapeDtypeStruct((slots // LANES, LANES), jnp.int32),
            jax.ShapeDtypeStruct((count // LANES, LANES), jnp.float32),
            jax.ShapeDtypeStruct((LANES, 2 * PADH), jnp.float32),
        ),
        in_specs=[pl.BlockSpec(memory_space=pltpu.SMEM), vm, vm, vm, vm],
        out_specs=(vm, vm, vm),
        cost_estimate=pl.CostEstimate(
            flops=int(4e-6 * 1.1e15), bytes_accessed=8 * 2**20, transcendentals=0
        ),
        compiler_params=pltpu.CompilerParams(vmem_limit_bytes=8 << 20),
        name="index_tables",
    )(
        order,
        new_index.reshape(-1, LANES),
        jacobian.reshape(-1, LANES),
        order.reshape(-1, LANES),
        minv,
    )


PADH = 56
BINS = 512


def project_kernel(
    recv_ref, m_ref, target_ref, minv_ref, jac_ref, out_ref, coef_ref, y0, y1, lhs0, lhs1, acc0, acc1
):
    turn = pl.program_id(0)
    folds = acc0.shape[0] // (2 * PADH)
    half = jnp.bfloat16
    single = jnp.float32

    @pl.when(turn == 0)
    def _():
        for ref in (acc0, acc1, y0, y1):
            ref[...] = jnp.zeros_like(ref)

    low = lax.broadcasted_iota(jnp.int32, (8, LANES), 1) < 64
    first = pl.multiple_of(turn * (8 * ROWS), 8)
    for r in range(HALF):
        even = recv_ref[pl.ds(first + r, 8, stride=ROWS), :]
        odd = recv_ref[pl.ds(first + HALF + r, 8, stride=ROWS), :]
        coef_ref[r] = jnp.where(low, even, pltpu.roll(odd, 64, 1))
        coef_ref[r + HALF] = jnp.where(low, pltpu.roll(even, 64, 1), odd)
    slots = 8 * LANES
    target = jnp.concatenate([target_ref[g : g + 1, :] for g in range(8)], axis=1)
    fold = target // BINS
    bins = lax.broadcasted_iota(jnp.int32, (256, slots), 0).astype(single).astype(half)
    within = target & (BINS - 1)
    parts = []
    for h in range(BINS // 256):
        wanted = (within - 256 * h).astype(single).astype(half)
        parts.append(jnp.where(bins == wanted, jnp.array(1, half), jnp.array(0, half)))
    hot = jnp.concatenate(parts, axis=0)
    tile = 5
    span = MODES // 2

    def apply(y_ref, start):
        for m0 in range(start, start + span, tile):
            accs = [None] * (tile * VARS)
            for k in range(MODES):
                coefs = [coef_ref[v * MODES + k] for v in range(VARS)]
                for i in range(tile):
                    entry = m_ref[0, (m0 + i) * MODES + k]
                    for v in range(VARS):
                        term = entry * coefs[v]
                        old = accs[i * VARS + v]
                        accs[i * VARS + v] = term if old is None else old + term
            for i in range(tile):
                for v in range(VARS):
                    f = v * span + m0 - start + i
                    y_ref[pl.ds((f // 8) * 64 + f % 8, 8, stride=8), :] = accs[i * VARS + v]

    def widen(y_ref, lhs_ref):
        rows = []
        for fb in range(PADH // 8):
            rows.append(
                jnp.concatenate(
                    [y_ref[(fb * 8 + g) * 8 : (fb * 8 + g) * 8 + 8, :] for g in range(8)], axis=1
                )
            )
        y = jnp.concatenate(rows, axis=0)
        high = y.astype(half).astype(single)
        both = jnp.concatenate([high, y - high], axis=0).astype(half)
        for a in range(folds):
            keep = jnp.where(fold == a, 1.0, 0.0).astype(half)
            lhs_ref[a * 2 * PADH : (a + 1) * 2 * PADH, :] = both * keep

    def deposit(lhs_ref, acc_ref):
        acc_ref[...] += lax.dot_general(
            lhs_ref[...], hot, (((1,), (1,)), ((), ())), preferred_element_type=single
        )

    apply(y0, 0)
    widen(y0, lhs0)
    deposit(lhs0, acc0)
    apply(y1, span)
    widen(y1, lhs1)
    deposit(lhs1, acc1)

    @pl.when(turn == pl.num_programs(0) - 1)
    def _():
        minv = minv_ref[...]
        minv_h = minv.astype(half).astype(single)
        left = jnp.concatenate([minv_h, minv_h, minv - minv_h], axis=1).astype(half)
        scale = 1.0 / jac_ref[...]
        for a in range(folds):
            base = a * 2 * PADH
            rhs = jnp.concatenate(
                [
                    ref[base : base + PADH, :] + ref[base + PADH : base + 2 * PADH, :]
                    for ref in (acc0, acc1)
                ],
                axis=0,
            )
            rhs_h = rhs.astype(half).astype(single)
            right = jnp.concatenate([rhs_h, rhs - rhs_h, rhs_h], axis=0).astype(half)
            done = jnp.dot(left, right, preferred_element_type=single)
            done = done * scale[:, a * BINS : (a + 1) * BINS]
            for j in range(BINS // LANES):
                out_ref[a * BINS + j * LANES : a * BINS + (j + 1) * LANES, :] = done[
                    :, j * LANES : (j + 1) * LANES
                ].T


def project(received, matrix, target, minv, jac):
    blocks = matrix.shape[0]
    count = jac.shape[1]
    folds = count // BINS
    return pl.pallas_call(
        project_kernel,
        grid=(blocks,),
        out_shape=jax.ShapeDtypeStruct((count, LANES), jnp.float32),
        in_specs=[
            pl.BlockSpec(memory_space=pltpu.VMEM),
            pl.BlockSpec((1, MODES * MODES, 8, LANES), lambda i: (i, 0, 0, 0)),
            pl.BlockSpec((8, LANES), lambda i: (i, 0)),
            pl.BlockSpec((LANES, 2 * PADH), lambda i: (0, 0)),
            pl.BlockSpec((1, count), lambda i: (0, 0)),
        ],
        out_specs=pl.BlockSpec((count, LANES), lambda i: (0, 0)),
        scratch_shapes=[
            pltpu.VMEM((ROWS, 8, LANES), jnp.float32),
            pltpu.VMEM((PADH * 8, LANES), jnp.float32),
            pltpu.VMEM((PADH * 8, LANES), jnp.float32),
            pltpu.VMEM((folds * 2 * PADH, 8 * LANES), jnp.bfloat16),
            pltpu.VMEM((folds * 2 * PADH, 8 * LANES), jnp.bfloat16),
            pltpu.VMEM((folds * 2 * PADH, BINS), jnp.float32),
            pltpu.VMEM((folds * 2 * PADH, BINS), jnp.float32),
        ],
        compiler_params=pltpu.CompilerParams(vmem_limit_bytes=44 << 20),
        name="project",
    )(received, matrix, target, minv, jac)


def local(old_coef, old_index, pair_count, new_index, old_points, new_points, weights, jacobian,
          minv_ref, send_order):
    axes = ("dom", "sub")
    devices = lax.axis_size(axes)
    outgoing = gather(old_coef, old_index, pair_count, lax.axis_size("sub"))
    outgoing = outgoing.reshape(devices, HALF // 2, 2, LANES)
    received = lax.all_to_all(outgoing, axes, split_axis=0, concat_axis=0, tiled=True)
    received = received.reshape(devices * HALF, LANES)
    target, jac, minv = index_tables(send_order[0], new_index, jacobian, minv_ref)
    old_points, new_points, target = lax.optimization_barrier((old_points, new_points, target))
    matrix = moment_matrix(old_points, new_points, weights)
    leaving = project(received, matrix, target, minv, jac.reshape(1, -1))
    leaving = leaving.reshape(devices, -1, LANES)
    arrived = lax.all_to_all(leaving, axes, split_axis=0, concat_axis=0, tiled=True)
    return arrived.reshape(-1, LANES)[:, :ROWS].T


def solution(mesh):
    placed = (
        P(None, ("dom", "sub")),
        P(("dom", "sub")),
        P(),
        P(("dom", "sub")),
        P(None, ("dom", "sub")),
        P(None, ("dom", "sub")),
        P(("dom", "sub")),
        P(("dom", "sub")),
        P(),
        P(("dom", "sub"), None),
    )
    return jax.shard_map(
        local, mesh=mesh, in_specs=placed, out_specs=P(None, ("dom", "sub")), check_vma=False
    )
```

```python
import functools
import jax
import jax.numpy as jnp
from jax import lax
from jax.experimental import pallas as pl
from jax.experimental.pallas import tpu as pltpu
from jax.sharding import PartitionSpec as P

VARS = 5
MODES = 20
ROWS = 100
HALF = 50
QUAD = 24
CAP = 64
LANES = 128


def gather_kernel(
    subs, idx_hbm, cnt_hbm, coef_hbm, out_ref, tab_ref, buf_ref, coef_ref, idx_ref, cnt_ref, sems
):
    part = pl.program_id(0)
    rank = lax.axis_index("dom") * subs + lax.axis_index("sub")
    myself = rank % 8
    width = coef_ref.shape[1]
    pairs = buf_ref.shape[0] // LANES
    lane = lax.broadcasted_iota(jnp.int32, (1, LANES), 1)
    low = lane < 64

    @pl.when(part == 0)
    def _():
        cuts = 4
        span = width // cuts
        wide = [
            pltpu.make_async_copy(
                coef_hbm.at[:, pl.ds(c * span, span)],
                coef_ref.at[:, pl.ds(c * span, span)],
                sems.at[c],
            )
            for c in range(cuts)
        ]
        start = pl.multiple_of(rank - myself, 8)
        small = [
            pltpu.make_async_copy(idx_hbm, idx_ref, sems.at[cuts]),
            pltpu.make_async_copy(cnt_hbm.at[pl.ds(start, 8), :], cnt_ref, sems.at[cuts + 1]),
        ]
        for copy in wide[:1] + small + wide[1:]:
            copy.start()
        pad = jnp.zeros((64 - HALF, LANES), jnp.float32)

        def build(j, carry):
            start = pl.multiple_of(j * LANES, LANES)
            block = coef_ref[:, pl.ds(start, LANES)]
            wide = jnp.concatenate([block[:HALF], pad, block[HALF:], pad], axis=0)
            tab_ref[pl.ds(start, LANES), :] = wide.T
            return carry

        for c in range(cuts):
            wide[c].wait()
            lax.fori_loop(c * (span // LANES), (c + 1) * (span // LANES), build, 0, unroll=4)
        for copy in small:
            copy.wait()

    def fetch(t, carry):
        base = pl.multiple_of(t * LANES, LANES)
        first = (part * pairs + t) * LANES
        for j in range(LANES):
            buf_ref[pl.ds(base + j, 1), :] = tab_ref[pl.ds(idx_ref[first + j], 1), :]
        return carry

    lax.fori_loop(0, pairs, fetch, 0)

    turned = [buf_ref[u * LANES : (u + 1) * LANES, :].T for u in range(pairs)]
    for u in range(pairs):
        pair = part * pairs + u
        limit = jnp.where(low, cnt_ref[myself, 2 * pair], cnt_ref[myself, 2 * pair + 1] + 64)
        live = lane < limit
        first = jnp.where(live, turned[u][:HALF], 0.0)
        second = jnp.where(live, turned[u][64 : 64 + HALF], 0.0)
        out_ref[u * ROWS : u * ROWS + HALF, :] = jnp.where(low, first, pltpu.roll(second, 64, 1))
        out_ref[u * ROWS + HALF : (u + 1) * ROWS, :] = jnp.where(
            low, pltpu.roll(first, 64, 1), second
        )


def gather(old_coef, old_index, pair_count, subs, steps=4):
    slots = old_index.shape[0]
    rows, width = old_coef.shape
    total = slots // CAP * HALF
    return pl.pallas_call(
        functools.partial(gather_kernel, subs),
        grid=(steps,),
        out_shape=jax.ShapeDtypeStruct((total, LANES), jnp.float32),
        in_specs=[pl.BlockSpec(memory_space=pl.ANY)] * 3,
        out_specs=pl.BlockSpec((total // steps, LANES), lambda i: (i, 0)),
        scratch_shapes=[
            pltpu.VMEM((width, LANES), jnp.float32),
            pltpu.VMEM((slots // steps, LANES), jnp.float32),
            pltpu.VMEM((rows, width), jnp.float32),
            pltpu.SMEM((slots,), jnp.int32),
            pltpu.SMEM((8, pair_count.shape[1]), jnp.int32),
            pltpu.SemaphoreType.DMA((6,)),
        ],
        name="gather",
    )(old_index, pair_count, old_coef)


def monomials(first, second, third):
    unit = None
    fp = [unit, first, first * first]
    fp.append(fp[2] * first)
    sp = [unit, second, second * second]
    sp.append(sp[2] * second)
    tp = [unit, third, third * third]
    tp.append(tp[2] * third)
    rows = []
    for degree in range(4):
        for a in range(degree, -1, -1):
            for b in range(degree - a, -1, -1):
                out = None
                for term in (fp[a], sp[b], tp[degree - a - b]):
                    if term is not None:
                        out = term if out is None else out * term
                rows.append(out)
    return rows


def moment_kernel(old_ref, new_ref, w_ref, out_ref, po_ref, pn_ref):
    def basis(q, carry):
        weight = w_ref[q]
        old = monomials(*[old_ref[a, q] for a in range(3)])
        new = monomials(*[new_ref[a, q] for a in range(3)])
        for k in range(1, MODES):
            pn_ref[q, k] = new[k] * weight
            if k > 3:
                po_ref[q, k] = old[k]
        return carry

    lax.fori_loop(0, QUAD, basis, 0, unroll=2)
    tile = 5
    zero = jnp.zeros((8, LANES), jnp.float32)

    def weighted(q, m):
        return w_ref[q] if m == 0 else pn_ref[q, m]

    def plain(q, k):
        if k == 0:
            return None
        return old_ref[k - 1, q] if k < 4 else po_ref[q, k]

    for m0 in range(0, MODES, tile):
        for k0 in range(0, MODES, tile):

            def add(q, accs):
                left = [weighted(q, m0 + i) for i in range(tile)]
                right = [plain(q, k0 + j) for j in range(tile)]
                return tuple(
                    accs[i * tile + j] + (left[i] if right[j] is None else left[i] * right[j])
                    for i in range(tile)
                    for j in range(tile)
                )

            accs = lax.fori_loop(0, QUAD, add, (zero,) * (tile * tile), unroll=12)
            for i in range(tile):
                for j in range(tile):
                    out_ref[0, (m0 + i) * MODES + k0 + j] = accs[i * tile + j]


def moment_matrix(old_points, new_points, weights):
    groups = weights.shape[0] // QUAD // LANES
    blocks = groups // 8
    shape = (3, QUAD, groups, LANES)
    return pl.pallas_call(
        moment_kernel,
        grid=(blocks,),
        out_shape=jax.ShapeDtypeStruct((blocks, MODES * MODES, 8, LANES), jnp.float32),
        in_specs=[
            pl.BlockSpec((3, QUAD, 8, LANES), lambda i: (0, 0, i, 0)),
            pl.BlockSpec((3, QUAD, 8, LANES), lambda i: (0, 0, i, 0)),
            pl.BlockSpec((QUAD, 8, LANES), lambda i: (0, i, 0)),
        ],
        out_specs=pl.BlockSpec((1, MODES * MODES, 8, LANES), lambda i: (i, 0, 0, 0)),
        scratch_shapes=[
            pltpu.VMEM((QUAD, MODES, 8, LANES), jnp.float32),
            pltpu.VMEM((QUAD, MODES, 8, LANES), jnp.float32),
        ],
        cost_estimate=pl.CostEstimate(
            flops=int(20e-6 * 1.1e15), bytes_accessed=40 * 2**20, transcendentals=0
        ),
        name="moment_matrix",
    )(old_points.reshape(shape), new_points.reshape(shape), weights.reshape(shape[1:]))


def index_kernel(order_s, index_ref, jac_ref, order_ref, minv_ref, target_ref, jacp_ref, wide_ref):
    wide_ref[...] = jnp.zeros_like(wide_ref)
    span = MODES // 2
    for v in range(VARS):
        for h in range(2):
            start = h * PADH + v * span
            wide_ref[v * MODES : (v + 1) * MODES, start : start + span] = minv_ref[
                :, h * span : (h + 1) * span
            ]
    rows = jac_ref.shape[0]
    place = lax.broadcasted_iota(jnp.int32, (rows, LANES), 0) * LANES + lax.broadcasted_iota(
        jnp.int32, (rows, LANES), 1
    )

    def invert(p, inverse):
        return jnp.where(place == order_s[p], p, inverse)

    inverse = lax.fori_loop(
        0, rows * LANES, invert, jnp.zeros((rows, LANES), jnp.int32), unroll=8
    )

    def look(table, index):
        low = index & (LANES - 1)
        high = index >> 7
        found = jnp.zeros(index.shape, table.dtype)
        for r in range(rows):
            row = jnp.broadcast_to(table[r : r + 1], index.shape)
            found = jnp.where(high == r, jnp.take_along_axis(row, low, axis=1), found)
        return found

    for g in range(index_ref.shape[0] // 8):
        target_ref[8 * g : 8 * g + 8, :] = look(inverse, index_ref[8 * g : 8 * g + 8, :])
    jac = jac_ref[...]
    for g in range(rows // 8):
        jacp_ref[8 * g : 8 * g + 8, :] = look(jac, order_ref[8 * g : 8 * g + 8, :])


def index_tables(order, new_index, jacobian, minv):
    slots = new_index.shape[0]
    count = order.shape[0]
    vm = pl.BlockSpec(memory_space=pltpu.VMEM)
    return pl.pallas_call(
        index_kernel,
        out_shape=(
            jax.ShapeDtypeStruct((slots // LANES, LANES), jnp.int32),
            jax.ShapeDtypeStruct((count // LANES, LANES), jnp.float32),
            jax.ShapeDtypeStruct((LANES, 2 * PADH), jnp.float32),
        ),
        in_specs=[pl.BlockSpec(memory_space=pltpu.SMEM), vm, vm, vm, vm],
        out_specs=(vm, vm, vm),
        cost_estimate=pl.CostEstimate(
            flops=int(4e-6 * 1.1e15), bytes_accessed=8 * 2**20, transcendentals=0
        ),
        compiler_params=pltpu.CompilerParams(vmem_limit_bytes=8 << 20),
        name="index_tables",
    )(
        order,
        new_index.reshape(-1, LANES),
        jacobian.reshape(-1, LANES),
        order.reshape(-1, LANES),
        minv,
    )


PADH = 56
SHARE = 16
TALL = 13
CUT = 25
BINS = 512


def project_kernel(
    recv_ref, m_ref, target_ref, minv_ref, jac_ref, out_ref, coef_ref, y0, y1, lhs0, lhs1, acc0, acc1, turned_ref
):
    turn = pl.program_id(0)
    folds = acc0.shape[0] // (2 * PADH)
    half = jnp.bfloat16
    single = jnp.float32

    @pl.when(turn == 0)
    def _():
        for ref in (acc0, acc1, y0, y1):
            ref[...] = jnp.zeros_like(ref)

    low = lax.broadcasted_iota(jnp.int32, (8, LANES), 1) < 64
    first = pl.multiple_of(turn * (8 * ROWS), 8)
    for r in range(HALF):
        even = recv_ref[pl.ds(first + r, 8, stride=ROWS), :]
        odd = recv_ref[pl.ds(first + HALF + r, 8, stride=ROWS), :]
        coef_ref[r] = jnp.where(low, even, pltpu.roll(odd, 64, 1))
        coef_ref[r + HALF] = jnp.where(low, pltpu.roll(even, 64, 1), odd)
    slots = 8 * LANES
    target = jnp.concatenate([target_ref[g : g + 1, :] for g in range(8)], axis=1)
    fold = target // BINS
    bins = lax.broadcasted_iota(jnp.int32, (256, slots), 0).astype(single).astype(half)
    within = target & (BINS - 1)
    parts = []
    for h in range(BINS // 256):
        wanted = (within - 256 * h).astype(single).astype(half)
        parts.append(jnp.where(bins == wanted, jnp.array(1, half), jnp.array(0, half)))
    hot = jnp.concatenate(parts, axis=0)
    tile = 2
    span = MODES // 2

    def apply(y_ref, start):
        for m0 in range(start, start + span, tile):
            accs = [None] * (tile * VARS)
            for k in range(MODES):
                coefs = [coef_ref[v * MODES + k] for v in range(VARS)]
                for i in range(tile):
                    entry = m_ref[0, (m0 + i) * MODES + k]
                    for v in range(VARS):
                        term = entry * coefs[v]
                        old = accs[i * VARS + v]
                        accs[i * VARS + v] = term if old is None else old + term
            for i in range(tile):
                for v in range(VARS):
                    f = v * span + m0 - start + i
                    y_ref[pl.ds((f // 8) * 64 + f % 8, 8, stride=8), :] = accs[i * VARS + v]

    def widen(y_ref, lhs_ref):
        rows = []
        for fb in range(PADH // 8):
            rows.append(
                jnp.concatenate(
                    [y_ref[(fb * 8 + g) * 8 : (fb * 8 + g) * 8 + 8, :] for g in range(8)], axis=1
                )
            )
        y = jnp.concatenate(rows, axis=0)
        high = y.astype(half).astype(single)
        both = jnp.concatenate([high, y - high], axis=0).astype(half)
        for a in range(folds):
            keep = jnp.where(fold == a, 1.0, 0.0).astype(half)
            lhs_ref[a * 2 * PADH : (a + 1) * 2 * PADH, :] = both * keep

    def deposit(lhs_ref, acc_ref):
        acc_ref[...] += lax.dot_general(
            lhs_ref[...], hot, (((1,), (1,)), ((), ())), preferred_element_type=single
        )

    apply(y0, 0)
    widen(y0, lhs0)
    deposit(lhs0, acc0)
    apply(y1, span)
    widen(y1, lhs1)
    deposit(lhs1, acc1)

    @pl.when(turn == pl.num_programs(0) - 1)
    def _():
        minv = minv_ref[...]
        minv_h = minv.astype(half).astype(single)
        left = jnp.concatenate([minv_h, minv_h, minv - minv_h], axis=1).astype(half)
        scale = 1.0 / jac_ref[...]
        for a in range(folds):
            base = a * 2 * PADH
            rhs = jnp.concatenate(
                [
                    ref[base : base + PADH, :] + ref[base + PADH : base + 2 * PADH, :]
                    for ref in (acc0, acc1)
                ],
                axis=0,
            )
            rhs_h = rhs.astype(half).astype(single)
            right = jnp.concatenate([rhs_h, rhs - rhs_h, rhs_h], axis=0).astype(half)
            done = jnp.dot(left, right, preferred_element_type=single)
            done = done * scale[:, a * BINS : (a + 1) * BINS]
            for j in range(BINS // LANES):
                turned_ref[a * BINS + j * LANES : a * BINS + (j + 1) * LANES, :] = done[
                    :, j * LANES : (j + 1) * LANES
                ].T
        lane = lax.broadcasted_iota(jnp.int32, (8, LANES), 1)
        for g in range(turned_ref.shape[0] // LANES):
            for i in range(SHARE - TALL):
                extra = turned_ref[pl.ds(g * LANES + TALL + i, 8, stride=SHARE), :]
                for c in range(4):
                    r = 4 * i + c
                    kept = turned_ref[pl.ds(g * LANES + r, 8, stride=SHARE), :]
                    moved = pltpu.roll(extra, ROWS - CUT * c, 1)
                    out_ref[pl.ds(g * 8 * TALL + r, 8, stride=TALL), :] = jnp.where(
                        lane < ROWS, kept, moved
                    )
            out_ref[pl.ds(g * 8 * TALL + TALL - 1, 8, stride=TALL), :] = turned_ref[
                pl.ds(g * LANES + TALL - 1, 8, stride=SHARE), :
            ]


def project(received, matrix, target, minv, jac):
    blocks = matrix.shape[0]
    count = jac.shape[1]
    folds = count // BINS
    return pl.pallas_call(
        project_kernel,
        grid=(blocks,),
        out_shape=jax.ShapeDtypeStruct((count // SHARE * TALL, LANES), jnp.float32),
        in_specs=[
            pl.BlockSpec(memory_space=pltpu.VMEM),
            pl.BlockSpec((1, MODES * MODES, 8, LANES), lambda i: (i, 0, 0, 0)),
            pl.BlockSpec((8, LANES), lambda i: (i, 0)),
            pl.BlockSpec((LANES, 2 * PADH), lambda i: (0, 0)),
            pl.BlockSpec((1, count), lambda i: (0, 0)),
        ],
        out_specs=pl.BlockSpec((count // SHARE * TALL, LANES), lambda i: (0, 0)),
        scratch_shapes=[
            pltpu.VMEM((ROWS, 8, LANES), jnp.float32),
            pltpu.VMEM((PADH * 8, LANES), jnp.float32),
            pltpu.VMEM((PADH * 8, LANES), jnp.float32),
            pltpu.VMEM((folds * 2 * PADH, 8 * LANES), jnp.bfloat16),
            pltpu.VMEM((folds * 2 * PADH, 8 * LANES), jnp.bfloat16),
            pltpu.VMEM((folds * 2 * PADH, BINS), jnp.float32),
            pltpu.VMEM((folds * 2 * PADH, BINS), jnp.float32),
            pltpu.VMEM((count, LANES), jnp.float32),
        ],
        compiler_params=pltpu.CompilerParams(vmem_limit_bytes=44 << 20),
        name="project",
    )(received, matrix, target, minv, jac)


def arrange_kernel(in_ref, out_ref, turned_ref):
    lane = lax.broadcasted_iota(jnp.int32, (8, LANES), 1)
    for g in range(out_ref.shape[1] // LANES):
        for i in range(SHARE - TALL):
            extra = jnp.zeros((8, LANES), jnp.float32)
            for c in range(4):
                r = 4 * i + c
                row = in_ref[pl.ds(g * 8 * TALL + r, 8, stride=TALL), :]
                turned_ref[pl.ds(g * LANES + r, 8, stride=SHARE), :] = row
                moved = pltpu.roll(row, LANES - ROWS + CUT * c, 1)
                extra = jnp.where((lane >= CUT * c) & (lane < CUT * (c + 1)), moved, extra)
            turned_ref[pl.ds(g * LANES + TALL + i, 8, stride=SHARE), :] = extra
        turned_ref[pl.ds(g * LANES + TALL - 1, 8, stride=SHARE), :] = in_ref[
            pl.ds(g * 8 * TALL + TALL - 1, 8, stride=TALL), :
        ]
    for g in range(out_ref.shape[1] // LANES):
        span = slice(g * LANES, (g + 1) * LANES)
        out_ref[:, span] = turned_ref[span, :].T[:ROWS]


def arrange(arrived):
    width = arrived.shape[0] // TALL * SHARE
    return pl.pallas_call(
        arrange_kernel,
        out_shape=jax.ShapeDtypeStruct((ROWS, width), jnp.float32),
        in_specs=[pl.BlockSpec(memory_space=pltpu.VMEM)],
        out_specs=pl.BlockSpec(memory_space=pltpu.VMEM),
        scratch_shapes=[pltpu.VMEM((width, LANES), jnp.float32)],
        compiler_params=pltpu.CompilerParams(vmem_limit_bytes=24 << 20),
        name="arrange",
    )(arrived)


def local(old_coef, old_index, pair_count, new_index, old_points, new_points, weights, jacobian,
          minv_ref, send_order):
    axes = ("dom", "sub")
    devices = lax.axis_size(axes)
    outgoing = gather(old_coef, old_index, pair_count, lax.axis_size("sub"))
    outgoing = outgoing.reshape(devices, HALF // 2, 2, LANES)
    received = lax.all_to_all(outgoing, axes, split_axis=0, concat_axis=0, tiled=True)
    received = received.reshape(devices * HALF, LANES)
    target, jac, minv = index_tables(send_order[0], new_index, jacobian, minv_ref)
    old_points, new_points, target = lax.optimization_barrier((old_points, new_points, target))
    matrix = moment_matrix(old_points, new_points, weights)
    leaving = project(received, matrix, target, minv, jac.reshape(1, -1))
    leaving = leaving.reshape(devices, TALL, 1, LANES)
    arrived = lax.all_to_all(leaving, axes, split_axis=0, concat_axis=0, tiled=True)
    return arrange(arrived.reshape(-1, LANES))


def solution(mesh):
    placed = (
        P(None, ("dom", "sub")),
        P(("dom", "sub")),
        P(),
        P(("dom", "sub")),
        P(None, ("dom", "sub")),
        P(None, ("dom", "sub")),
        P(("dom", "sub")),
        P(("dom", "sub")),
        P(),
        P(("dom", "sub"), None),
    )
    return jax.shard_map(
        local, mesh=mesh, in_specs=placed, out_specs=P(None, ("dom", "sub")), check_vma=False
    )
```

```python
import functools
import jax
import jax.numpy as jnp
from jax import lax
from jax.experimental import pallas as pl
from jax.experimental.pallas import tpu as pltpu
from jax.sharding import PartitionSpec as P

VARS = 5
MODES = 20
ROWS = 100
HALF = 50
QUAD = 24
CAP = 64
LANES = 128


def gather_kernel(
    subs, idx_hbm, cnt_hbm, coef_hbm, out_ref, tab_ref, buf_ref, coef_ref, idx_ref, cnt_ref, sems
):
    part = pl.program_id(0)
    rank = lax.axis_index("dom") * subs + lax.axis_index("sub")
    myself = rank % 8
    width = coef_ref.shape[1]
    pairs = buf_ref.shape[0] // LANES
    lane = lax.broadcasted_iota(jnp.int32, (1, LANES), 1)
    low = lane < 64

    @pl.when(part == 0)
    def _():
        cuts = 4
        span = width // cuts
        wide = [
            pltpu.make_async_copy(
                coef_hbm.at[:, pl.ds(c * span, span)],
                coef_ref.at[:, pl.ds(c * span, span)],
                sems.at[c],
            )
            for c in range(cuts)
        ]
        start = pl.multiple_of(rank - myself, 8)
        small = [
            pltpu.make_async_copy(idx_hbm, idx_ref, sems.at[cuts]),
            pltpu.make_async_copy(cnt_hbm.at[pl.ds(start, 8), :], cnt_ref, sems.at[cuts + 1]),
        ]
        for copy in wide[:1] + small + wide[1:]:
            copy.start()
        pad = jnp.zeros((64 - HALF, LANES), jnp.float32)

        def build(j, carry):
            start = pl.multiple_of(j * LANES, LANES)
            block = coef_ref[:, pl.ds(start, LANES)]
            wide = jnp.concatenate([block[:HALF], pad, block[HALF:], pad], axis=0)
            tab_ref[pl.ds(start, LANES), :] = wide.T
            return carry

        for c in range(cuts):
            wide[c].wait()
            lax.fori_loop(c * (span // LANES), (c + 1) * (span // LANES), build, 0, unroll=4)
        for copy in small:
            copy.wait()

    def fetch(t, carry):
        base = pl.multiple_of(t * LANES, LANES)
        first = (part * pairs + t) * LANES
        def take(begin, end):
            for j in range(begin, end):
                buf_ref[pl.ds(base + j, 1), :] = tab_ref[pl.ds(idx_ref[first + j], 1), :]

        for side in range(2):
            used = cnt_ref[myself, 2 * (part * pairs + t) + side]
            for begin, end in ((0, 40), (40, 64)):
                if begin == 0:
                    take(side * CAP, side * CAP + end)
                else:
                    pl.when(used > begin)(
                        functools.partial(take, side * CAP + begin, side * CAP + end)
                    )
        return carry

    lax.fori_loop(0, pairs, fetch, 0)

    turned = [buf_ref[u * LANES : (u + 1) * LANES, :].T for u in range(pairs)]
    for u in range(pairs):
        pair = part * pairs + u
        limit = jnp.where(low, cnt_ref[myself, 2 * pair], cnt_ref[myself, 2 * pair + 1] + 64)
        live = lane < limit
        first = jnp.where(live, turned[u][:HALF], 0.0)
        second = jnp.where(live, turned[u][64 : 64 + HALF], 0.0)
        out_ref[u * ROWS : u * ROWS + HALF, :] = jnp.where(low, first, pltpu.roll(second, 64, 1))
        out_ref[u * ROWS + HALF : (u + 1) * ROWS, :] = jnp.where(
            low, pltpu.roll(first, 64, 1), second
        )


def gather(old_coef, old_index, pair_count, subs, steps=4):
    slots = old_index.shape[0]
    rows, width = old_coef.shape
    total = slots // CAP * HALF
    return pl.pallas_call(
        functools.partial(gather_kernel, subs),
        grid=(steps,),
        out_shape=jax.ShapeDtypeStruct((total, LANES), jnp.float32),
        in_specs=[pl.BlockSpec(memory_space=pl.ANY)] * 3,
        out_specs=pl.BlockSpec((total // steps, LANES), lambda i: (i, 0)),
        scratch_shapes=[
            pltpu.VMEM((width, LANES), jnp.float32),
            pltpu.VMEM((slots // steps, LANES), jnp.float32),
            pltpu.VMEM((rows, width), jnp.float32),
            pltpu.SMEM((slots,), jnp.int32),
            pltpu.SMEM((8, pair_count.shape[1]), jnp.int32),
            pltpu.SemaphoreType.DMA((6,)),
        ],
        name="gather",
    )(old_index, pair_count, old_coef)


def monomials(first, second, third):
    unit = None
    fp = [unit, first, first * first]
    fp.append(fp[2] * first)
    sp = [unit, second, second * second]
    sp.append(sp[2] * second)
    tp = [unit, third, third * third]
    tp.append(tp[2] * third)
    rows = []
    for degree in range(4):
        for a in range(degree, -1, -1):
            for b in range(degree - a, -1, -1):
                out = None
                for term in (fp[a], sp[b], tp[degree - a - b]):
                    if term is not None:
                        out = term if out is None else out * term
                rows.append(out)
    return rows


def moment_kernel(old_ref, new_ref, w_ref, out_ref, po_ref, pn_ref):
    def basis(q, carry):
        weight = w_ref[q]
        old = monomials(*[old_ref[a, q] for a in range(3)])
        new = monomials(*[new_ref[a, q] for a in range(3)])
        for k in range(1, MODES):
            pn_ref[q, k] = new[k] * weight
            if k > 3:
                po_ref[q, k] = old[k]
        return carry

    lax.fori_loop(0, QUAD, basis, 0, unroll=2)
    tile = 5
    zero = jnp.zeros((8, LANES), jnp.float32)

    def weighted(q, m):
        return w_ref[q] if m == 0 else pn_ref[q, m]

    def plain(q, k):
        if k == 0:
            return None
        return old_ref[k - 1, q] if k < 4 else po_ref[q, k]

    for m0 in range(0, MODES, tile):
        for k0 in range(0, MODES, tile):

            def add(q, accs):
                left = [weighted(q, m0 + i) for i in range(tile)]
                right = [plain(q, k0 + j) for j in range(tile)]
                return tuple(
                    accs[i * tile + j] + (left[i] if right[j] is None else left[i] * right[j])
                    for i in range(tile)
                    for j in range(tile)
                )

            accs = lax.fori_loop(0, QUAD, add, (zero,) * (tile * tile), unroll=12)
            for i in range(tile):
                for j in range(tile):
                    out_ref[0, (m0 + i) * MODES + k0 + j] = accs[i * tile + j]


def moment_matrix(old_points, new_points, weights):
    groups = weights.shape[0] // QUAD // LANES
    blocks = groups // 8
    shape = (3, QUAD, groups, LANES)
    return pl.pallas_call(
        moment_kernel,
        grid=(blocks,),
        out_shape=jax.ShapeDtypeStruct((blocks, MODES * MODES, 8, LANES), jnp.float32),
        in_specs=[
            pl.BlockSpec((3, QUAD, 8, LANES), lambda i: (0, 0, i, 0)),
            pl.BlockSpec((3, QUAD, 8, LANES), lambda i: (0, 0, i, 0)),
            pl.BlockSpec((QUAD, 8, LANES), lambda i: (0, i, 0)),
        ],
        out_specs=pl.BlockSpec((1, MODES * MODES, 8, LANES), lambda i: (i, 0, 0, 0)),
        scratch_shapes=[
            pltpu.VMEM((QUAD, MODES, 8, LANES), jnp.float32),
            pltpu.VMEM((QUAD, MODES, 8, LANES), jnp.float32),
        ],
        cost_estimate=pl.CostEstimate(
            flops=int(20e-6 * 1.1e15), bytes_accessed=40 * 2**20, transcendentals=0
        ),
        name="moment_matrix",
    )(old_points.reshape(shape), new_points.reshape(shape), weights.reshape(shape[1:]))


def index_kernel(order_s, index_ref, jac_ref, order_ref, minv_ref, target_ref, jacp_ref, wide_ref):
    wide_ref[...] = jnp.zeros_like(wide_ref)
    span = MODES // 2
    for v in range(VARS):
        for h in range(2):
            start = h * PADH + v * span
            wide_ref[v * MODES : (v + 1) * MODES, start : start + span] = minv_ref[
                :, h * span : (h + 1) * span
            ]
    rows = jac_ref.shape[0]
    place = lax.broadcasted_iota(jnp.int32, (rows, LANES), 0) * LANES + lax.broadcasted_iota(
        jnp.int32, (rows, LANES), 1
    )

    def invert(p, inverse):
        return jnp.where(place == order_s[p], p, inverse)

    inverse = lax.fori_loop(
        0, rows * LANES, invert, jnp.zeros((rows, LANES), jnp.int32), unroll=8
    )

    def look(table, index):
        low = index & (LANES - 1)
        high = index >> 7
        found = jnp.zeros(index.shape, table.dtype)
        for r in range(rows):
            row = jnp.broadcast_to(table[r : r + 1], index.shape)
            found = jnp.where(high == r, jnp.take_along_axis(row, low, axis=1), found)
        return found

    for g in range(index_ref.shape[0] // 8):
        target_ref[8 * g : 8 * g + 8, :] = look(inverse, index_ref[8 * g : 8 * g + 8, :])
    jac = jac_ref[...]
    for g in range(rows // 8):
        jacp_ref[8 * g : 8 * g + 8, :] = look(jac, order_ref[8 * g : 8 * g + 8, :])


def index_tables(order, new_index, jacobian, minv):
    slots = new_index.shape[0]
    count = order.shape[0]
    vm = pl.BlockSpec(memory_space=pltpu.VMEM)
    return pl.pallas_call(
        index_kernel,
        out_shape=(
            jax.ShapeDtypeStruct((slots // LANES, LANES), jnp.int32),
            jax.ShapeDtypeStruct((count // LANES, LANES), jnp.float32),
            jax.ShapeDtypeStruct((LANES, 2 * PADH), jnp.float32),
        ),
        in_specs=[pl.BlockSpec(memory_space=pltpu.SMEM), vm, vm, vm, vm],
        out_specs=(vm, vm, vm),
        cost_estimate=pl.CostEstimate(
            flops=int(4e-6 * 1.1e15), bytes_accessed=8 * 2**20, transcendentals=0
        ),
        compiler_params=pltpu.CompilerParams(vmem_limit_bytes=8 << 20),
        name="index_tables",
    )(
        order,
        new_index.reshape(-1, LANES),
        jacobian.reshape(-1, LANES),
        order.reshape(-1, LANES),
        minv,
    )


PADH = 56
SHARE = 16
TALL = 13
CUT = 25
BINS = 512


def project_kernel(
    recv_ref, m_ref, target_ref, minv_ref, jac_ref, out_ref, coef_ref, y0, y1, lhs0, lhs1, acc0, acc1, turned_ref
):
    turn = pl.program_id(0)
    folds = acc0.shape[0] // (2 * PADH)
    half = jnp.bfloat16
    single = jnp.float32

    @pl.when(turn == 0)
    def _():
        for ref in (acc0, acc1, y0, y1):
            ref[...] = jnp.zeros_like(ref)

    low = lax.broadcasted_iota(jnp.int32, (8, LANES), 1) < 64
    first = pl.multiple_of(turn * (8 * ROWS), 8)
    for r in range(HALF):
        even = recv_ref[pl.ds(first + r, 8, stride=ROWS), :]
        odd = recv_ref[pl.ds(first + HALF + r, 8, stride=ROWS), :]
        coef_ref[r] = jnp.where(low, even, pltpu.roll(odd, 64, 1))
        coef_ref[r + HALF] = jnp.where(low, pltpu.roll(even, 64, 1), odd)
    slots = 8 * LANES
    target = jnp.concatenate([target_ref[g : g + 1, :] for g in range(8)], axis=1)
    fold = target // BINS
    bins = lax.broadcasted_iota(jnp.int32, (256, slots), 0).astype(single).astype(half)
    within = target & (BINS - 1)
    parts = []
    for h in range(BINS // 256):
        wanted = (within - 256 * h).astype(single).astype(half)
        parts.append(jnp.where(bins == wanted, jnp.array(1, half), jnp.array(0, half)))
    hot = jnp.concatenate(parts, axis=0)
    tile = 2
    span = MODES // 2

    def apply(y_ref, start):
        for m0 in range(start, start + span, tile):
            accs = [None] * (tile * VARS)
            for k in range(MODES):
                coefs = [coef_ref[v * MODES + k] for v in range(VARS)]
                for i in range(tile):
                    entry = m_ref[0, (m0 + i) * MODES + k]
                    for v in range(VARS):
                        term = entry * coefs[v]
                        old = accs[i * VARS + v]
                        accs[i * VARS + v] = term if old is None else old + term
            for i in range(tile):
                for v in range(VARS):
                    f = v * span + m0 - start + i
                    y_ref[pl.ds((f // 8) * 64 + f % 8, 8, stride=8), :] = accs[i * VARS + v]

    def widen(y_ref, lhs_ref):
        rows = []
        for fb in range(PADH // 8):
            rows.append(
                jnp.concatenate(
                    [y_ref[(fb * 8 + g) * 8 : (fb * 8 + g) * 8 + 8, :] for g in range(8)], axis=1
                )
            )
        y = jnp.concatenate(rows, axis=0)
        high = y.astype(half).astype(single)
        both = jnp.concatenate([high, y - high], axis=0).astype(half)
        for a in range(folds):
            keep = jnp.where(fold == a, 1.0, 0.0).astype(half)
            lhs_ref[a * 2 * PADH : (a + 1) * 2 * PADH, :] = both * keep

    def deposit(lhs_ref, acc_ref):
        acc_ref[...] += lax.dot_general(
            lhs_ref[...], hot, (((1,), (1,)), ((), ())), preferred_element_type=single
        )

    apply(y0, 0)
    widen(y0, lhs0)
    deposit(lhs0, acc0)
    apply(y1, span)
    widen(y1, lhs1)
    deposit(lhs1, acc1)

    @pl.when(turn == pl.num_programs(0) - 1)
    def _():
        minv = minv_ref[...]
        minv_h = minv.astype(half).astype(single)
        left = jnp.concatenate([minv_h, minv_h, minv - minv_h], axis=1).astype(half)
        scale = 1.0 / jac_ref[...]
        for a in range(folds):
            base = a * 2 * PADH
            rhs = jnp.concatenate(
                [
                    ref[base : base + PADH, :] + ref[base + PADH : base + 2 * PADH, :]
                    for ref in (acc0, acc1)
                ],
                axis=0,
            )
            rhs_h = rhs.astype(half).astype(single)
            right = jnp.concatenate([rhs_h, rhs - rhs_h, rhs_h], axis=0).astype(half)
            done = jnp.dot(left, right, preferred_element_type=single)
            done = done * scale[:, a * BINS : (a + 1) * BINS]
            for j in range(BINS // LANES):
                turned_ref[a * BINS + j * LANES : a * BINS + (j + 1) * LANES, :] = done[
                    :, j * LANES : (j + 1) * LANES
                ].T
        lane = lax.broadcasted_iota(jnp.int32, (8, LANES), 1)
        for g in range(turned_ref.shape[0] // LANES):
            for i in range(SHARE - TALL):
                extra = turned_ref[pl.ds(g * LANES + TALL + i, 8, stride=SHARE), :]
                for c in range(4):
                    r = 4 * i + c
                    kept = turned_ref[pl.ds(g * LANES + r, 8, stride=SHARE), :]
                    moved = pltpu.roll(extra, ROWS - CUT * c, 1)
                    out_ref[pl.ds(g * 8 * TALL + r, 8, stride=TALL), :] = jnp.where(
                        lane < ROWS, kept, moved
                    )
            out_ref[pl.ds(g * 8 * TALL + TALL - 1, 8, stride=TALL), :] = turned_ref[
                pl.ds(g * LANES + TALL - 1, 8, stride=SHARE), :
            ]


def project(received, matrix, target, minv, jac):
    blocks = matrix.shape[0]
    count = jac.shape[1]
    folds = count // BINS
    return pl.pallas_call(
        project_kernel,
        grid=(blocks,),
        out_shape=jax.ShapeDtypeStruct((count // SHARE * TALL, LANES), jnp.float32),
        in_specs=[
            pl.BlockSpec(memory_space=pltpu.VMEM),
            pl.BlockSpec((1, MODES * MODES, 8, LANES), lambda i: (i, 0, 0, 0)),
            pl.BlockSpec((8, LANES), lambda i: (i, 0)),
            pl.BlockSpec((LANES, 2 * PADH), lambda i: (0, 0)),
            pl.BlockSpec((1, count), lambda i: (0, 0)),
        ],
        out_specs=pl.BlockSpec((count // SHARE * TALL, LANES), lambda i: (0, 0)),
        scratch_shapes=[
            pltpu.VMEM((ROWS, 8, LANES), jnp.float32),
            pltpu.VMEM((PADH * 8, LANES), jnp.float32),
            pltpu.VMEM((PADH * 8, LANES), jnp.float32),
            pltpu.VMEM((folds * 2 * PADH, 8 * LANES), jnp.bfloat16),
            pltpu.VMEM((folds * 2 * PADH, 8 * LANES), jnp.bfloat16),
            pltpu.VMEM((folds * 2 * PADH, BINS), jnp.float32),
            pltpu.VMEM((folds * 2 * PADH, BINS), jnp.float32),
            pltpu.VMEM((count, LANES), jnp.float32),
        ],
        compiler_params=pltpu.CompilerParams(vmem_limit_bytes=44 << 20),
        name="project",
    )(received, matrix, target, minv, jac)


def arrange_kernel(in_ref, out_ref, turned_ref):
    lane = lax.broadcasted_iota(jnp.int32, (8, LANES), 1)
    for g in range(out_ref.shape[1] // LANES):
        for i in range(SHARE - TALL):
            extra = jnp.zeros((8, LANES), jnp.float32)
            for c in range(4):
                r = 4 * i + c
                row = in_ref[pl.ds(g * 8 * TALL + r, 8, stride=TALL), :]
                turned_ref[pl.ds(g * LANES + r, 8, stride=SHARE), :] = row
                moved = pltpu.roll(row, LANES - ROWS + CUT * c, 1)
                extra = jnp.where((lane >= CUT * c) & (lane < CUT * (c + 1)), moved, extra)
            turned_ref[pl.ds(g * LANES + TALL + i, 8, stride=SHARE), :] = extra
        turned_ref[pl.ds(g * LANES + TALL - 1, 8, stride=SHARE), :] = in_ref[
            pl.ds(g * 8 * TALL + TALL - 1, 8, stride=TALL), :
        ]
    for g in range(out_ref.shape[1] // LANES):
        span = slice(g * LANES, (g + 1) * LANES)
        out_ref[:, span] = turned_ref[span, :].T[:ROWS]


def arrange(arrived):
    width = arrived.shape[0] // TALL * SHARE
    return pl.pallas_call(
        arrange_kernel,
        out_shape=jax.ShapeDtypeStruct((ROWS, width), jnp.float32),
        in_specs=[pl.BlockSpec(memory_space=pltpu.VMEM)],
        out_specs=pl.BlockSpec(memory_space=pltpu.VMEM),
        scratch_shapes=[pltpu.VMEM((width, LANES), jnp.float32)],
        compiler_params=pltpu.CompilerParams(vmem_limit_bytes=24 << 20),
        name="arrange",
    )(arrived)


def local(old_coef, old_index, pair_count, new_index, old_points, new_points, weights, jacobian,
          minv_ref, send_order):
    axes = ("dom", "sub")
    devices = lax.axis_size(axes)
    outgoing = gather(old_coef, old_index, pair_count, lax.axis_size("sub"))
    outgoing = outgoing.reshape(devices, HALF // 2, 2, LANES)
    received = lax.all_to_all(outgoing, axes, split_axis=0, concat_axis=0, tiled=True)
    received = received.reshape(devices * HALF, LANES)
    target, jac, minv = index_tables(send_order[0], new_index, jacobian, minv_ref)
    old_points, new_points, target = lax.optimization_barrier((old_points, new_points, target))
    matrix = moment_matrix(old_points, new_points, weights)
    leaving = project(received, matrix, target, minv, jac.reshape(1, -1))
    leaving = leaving.reshape(devices, TALL, 1, LANES)
    arrived = lax.all_to_all(leaving, axes, split_axis=0, concat_axis=0, tiled=True)
    return arrange(arrived.reshape(-1, LANES))


def solution(mesh):
    placed = (
        P(None, ("dom", "sub")),
        P(("dom", "sub")),
        P(),
        P(("dom", "sub")),
        P(None, ("dom", "sub")),
        P(None, ("dom", "sub")),
        P(("dom", "sub")),
        P(("dom", "sub")),
        P(),
        P(("dom", "sub"), None),
    )
    return jax.shard_map(
        local, mesh=mesh, in_specs=placed, out_specs=P(None, ("dom", "sub")), check_vma=False
    )
```
